32 devices in a mesh: ens: 2 (over y), mem: 4 (over x, core), lon: 4 (over z).
Axes of the slice: x: 2, y: 2, z: 4, core: 2. Of those that a mesh axis runs over, the one named last changes fastest.
Arguments:
- initial_state: float32 [8, 4, 4, 256, 128], P(('ens', 'mem'), None, None, 'lon'), parts along dimension 0, may hold values from -1.25 to 1.25
- ancestor: int32 [8], P(('ens', 'mem')), parts along dimension 0, may hold values from 0 to 3
- selector: int32 [8], P(('ens', 'mem')), parts along dimension 0, may hold values from 0 to 3
- perturbations: float32 [8, 4, 4, 256, 128], P('ens', None, None, 'lon'), parts along dimension 0, may hold values from -0.5 to 0.5
- diffusivity: float32 [4, 256, 128], P(None, 'lon'), may hold values from 0.05 to 0.3
- region_weight: float32 [256, 128], P('lon'), may hold values from 0.3 to 27, as said below
Outputs:
- final_state: float32 [8, 4, 4, 256, 128], P(('ens', 'mem'), None, None, 'lon'), parts along dimension 0
- actions: float32 [8, 2], P(('ens', 'mem')), parts along dimension 0
The draws below stay inside these ranges and needn't reach their ends.
There are 2 independent parts, one for each index of `ens`. The reference program is written for one: setup_inputs(seed, part) draws one part's arguments, and reference() takes and returns one part's arrays. A program takes and returns all parts, laid end to end along the dimension named above; an argument that names none is the same for every part. Nothing has to cross between parts.
Inputs may be any that keep to these rules, and one draw needn't show every extreme that they name: `region_weight`: Positive.
All inputs are finite; a program needn't handle non-finite values.
Results may differ from the reference program's by a relative error of at most 0.0001.
Values sent between devices are 32-bit elements; how exact they have to be, the bound alone decides.
A program may use at most 64 MiB of HBM per device.

```python
import math
import jax
import jax.numpy as jnp
import numpy as np

FIELDS = 4
LAT = 128
LEV = 4
NPERT = 4
STEPS = 3
LON = 256
MEMBERS = 4


def draw_region_weight(key, part):
    base = jax.random.uniform(key, (LON, LAT), jnp.float32, jnp.log(0.3), jnp.log(3.0))
    ramp = jnp.log(3.0) * jnp.arange(LON, dtype=jnp.float32)[:, None] / LON
    return jnp.exp(base + ramp)


def with_ends(entries, own_key, low, top_value):
    longest = entries.shape.index(max(entries.shape))
    spots = []
    for shift in (0, 1):
        where = [jax.random.randint(jax.random.fold_in(own_key, axis), (), 0, length) for axis, length in enumerate(entries.shape)]
        where[longest] = (where[longest] + shift) % entries.shape[longest]
        spots.append(tuple(where))
    return entries.at[spots[0]].set(low).at[spots[1]].set(top_value)


def block_scale(key, dims, pieces, low, high):
    factor_of = 1.0
    for dim, blocks in pieces:
        steps = jax.random.uniform(jax.random.fold_in(jax.random.fold_in(key, 6), dim), (blocks,), jnp.float32, low / len(pieces), high / len(pieces))
        factor_of = factor_of * jnp.repeat(jnp.exp(steps), dims[dim] // blocks).reshape((-1,) + (1,) * (len(dims) - 1 - dim))
    return factor_of


def rank_table(count, slope):
    weights = [(1 << 20) // math.isqrt(standing ** slope) + 1 for standing in range(1, count + 1)]
    width = 1 + sum(weights) // (1 << 30)
    return np.cumsum(np.array([max(1, weight // width) for weight in weights]))


def skewed_ids(stream_key, extent, count, slope):
    table = rank_table(count, slope)
    ticket = jax.random.randint(jax.random.fold_in(stream_key, 1), extent, 0, int(table[count - 1]))
    rank = jnp.searchsorted(jnp.asarray(table, jnp.int32), ticket, side="right")
    return jax.random.permutation(jax.random.fold_in(stream_key, 2), count)[rank].astype(jnp.int32)


def normal_values(rng, shape, width, limit, shards=(), held_as=jnp.bfloat16):
    array = jax.random.normal(rng, shape, jnp.float32) * width
    if len(shards) > 0:
        array = block_scale(rng, shape, shards, -0.22, 0.18) * array
    return jnp.clip(array, min=-limit, max=limit).astype(held_as)


def setup_inputs(seed: int = 0, part: int = 0) -> dict:
    key_list = jax.random.split(jax.random.key(seed), 7)
    own_keys = jax.random.split(jax.random.fold_in(key_list[6], part), 7)
    return {
        "initial_state": normal_values(own_keys[0], (MEMBERS, FIELDS, LEV, LON, LAT), 0.5, 1.25, ((0, 4), (3, 4)), jnp.float32),
        "ancestor": with_ends(skewed_ids(own_keys[1], (MEMBERS,), MEMBERS, 2), jax.random.fold_in(own_keys[1], 3), 0, MEMBERS - 1).astype(jnp.int32),
        "selector": with_ends(jax.random.randint(own_keys[2], (MEMBERS,), 0, NPERT), jax.random.fold_in(own_keys[2], 1), 0, NPERT - 1).astype(jnp.int32),
        "perturbations": normal_values(own_keys[3], (NPERT, FIELDS, LEV, LON, LAT), 0.2, 0.5, ((3, 4),), jnp.float32),
        "diffusivity": jnp.clip(0.05 + 0.25 * jax.random.uniform(key_list[4], (LEV, LON, LAT), jnp.float32) ** block_scale(key_list[4], (LEV, LON, LAT), ((1, 4),), -0.2, 0.2), 0.05, 0.3),
        "region_weight": draw_region_weight(jax.random.fold_in(key_list[6], 71), part),
    }


TIME_STEP = 0.2


def shifted_lat(tracer_field, upward_flux):
    if upward_flux:
        return jnp.concatenate([tracer_field[..., 1:], tracer_field[..., -1:]], axis=-1)
    return jnp.concatenate([tracer_field[..., :1], tracer_field[..., :-1]], axis=-1)


def cycle_pad(tracer_field):
    return jnp.concatenate([tracer_field[..., -1:, :], tracer_field, tracer_field[..., :1, :]], axis=-2)


def advance(padded, kappa_pad):
    centre = padded[..., 1:-1, :]
    west_cell = padded[..., :-2, :]
    east_cell = padded[..., 2:, :]
    south_cell = shifted_lat(centre, False)
    north_cell = shifted_lat(centre, True)
    kappa_mid = kappa_pad[..., 1:-1, :]
    kappa_west = 0.5 * (kappa_mid + kappa_pad[..., :-2, :])
    kappa_east = 0.5 * (kappa_mid + kappa_pad[..., 2:, :])
    kappa_south = 0.5 * (kappa_mid + shifted_lat(kappa_mid, False))
    kappa_north = 0.5 * (kappa_mid + shifted_lat(kappa_mid, True))
    zonal_wind = centre[:, 0:1]
    merid_wind = centre[:, 1:2]
    transport = (jnp.maximum(zonal_wind, 0.0) * (centre - west_cell)
                 + jnp.minimum(zonal_wind, 0.0) * (east_cell - centre)
                 + jnp.maximum(merid_wind, 0.0) * (centre - south_cell)
                 + jnp.minimum(merid_wind, 0.0) * (north_cell - centre))
    mixing = (kappa_east * (east_cell - centre) - kappa_west * (centre - west_cell)
              + kappa_north * (north_cell - centre) - kappa_south * (centre - south_cell))
    return centre + TIME_STEP * (mixing - transport)


def measure(tracer_field, clone_weight):
    thermal_field = tracer_field[:, 2]
    return jnp.sum(clone_weight * thermal_field * thermal_field, axis=(1, 2, 3))


def reference(initial_state, ancestor, selector, perturbations, diffusivity, region_weight):
    kappa_pad = cycle_pad(diffusivity)
    cell_count = LEV * LON * LAT

    def integrate_block(present_state):
        running = jnp.zeros((present_state.shape[0],), jnp.float32)
        for section in range(STEPS):
            present_state = advance(cycle_pad(present_state), kappa_pad)
            running = running + measure(present_state, region_weight) / cell_count
        return present_state, running

    middle, first_action = integrate_block(initial_state)
    cloned = jnp.take(middle, ancestor, axis=0) + jnp.take(perturbations, selector, axis=0)
    final_state, second_action = integrate_block(cloned)
    return final_state, jnp.stack([first_action, second_action], axis=1)
```

```python
import functools

import jax
import jax.numpy as jnp
from jax import lax
from jax.experimental import pallas as pl
from jax.experimental.pallas import tpu as pltpu
from jax.sharding import PartitionSpec as P

STEPS = 3
TIME_STEP = 0.2
EDGE = 8
VMEM_LIMIT = 60000000
MESH_ID = pl.DeviceIdType.MESH


def kernel(
    n, ring, anc_ref, sel_ref, init_ref, pert_ref, kap_ref, weight_ref, out_ref, act_ref,
    full, mid, noise, pert, noise_edge, noise_halo, kap, face, coef_mid, coef_end, weight,
    stage, ids, acc, part,
    x_send, x_recv, p_send, p_recv, z_send, z_recv, f_send, f_recv, o_send, o_recv,
    s_send, s_recv, local_sem, token,
):
    _, fields, levels, width, lat = init_ref.shape
    half = levels // 2
    rows = width + 2 * EDGE
    dyn = fields - 1
    pairs = n // 2
    top = width - EDGE
    mem = lax.axis_index("mem")
    lon = lax.axis_index("lon")
    core = lax.rem(mem, 2)
    base = mem - core
    twin = base + 1 - core
    east, west = lax.rem(lon + 1, ring), lax.rem(lon + ring - 1, ring)
    mine = core * half

    local = [
        pltpu.make_async_copy(
            init_ref.at[0, :, pl.ds(mine, half)],
            full.at[mem, :, :, pl.ds(EDGE, width)],
            local_sem.at[0],
        ),
        pltpu.make_async_copy(
            kap_ref.at[pl.ds(mine, half)], kap.at[:, pl.ds(EDGE, width)], local_sem.at[1]
        ),
        pltpu.make_async_copy(weight_ref, weight, local_sem.at[2]),
        pltpu.make_async_copy(pert_ref.at[:, :, pl.ds(mine, half)], pert, local_sem.at[3]),
    ]

    barrier = pltpu.get_barrier_semaphore()
    links = [(q, t) for q in range(1, pairs) for t in range(2)]

    def core_of(t):
        return core if t == 0 else 1 - core

    def target(q, t):
        return lax.rem(base + 2 * q, n) + core_of(t)

    def sender(q, t):
        return lax.rem(base + n - 2 * q, n) + core_of(t)

    for q, t in links + [(0, 1)]:
        pl.semaphore_signal(
            barrier, inc=1, device_id={"mem": target(q, t)}, device_id_type=MESH_ID
        )

    def toward(semaphore, up, t):
        @pl.when(lon < ring - 1 if up else lon > 0)
        def _():
            pl.semaphore_signal(
                semaphore,
                inc=1,
                device_id={"lon": east if up else west, "mem": target(0, t)},
                device_id_type=MESH_ID,
            )

    for t in range(2):
        toward(barrier, True, t)
        toward(barrier, False, t)
    for copy in local:
        copy.start()
    beside = jnp.where(lon > 0, 1, 0) + jnp.where(lon < ring - 1, 1, 0)
    pl.semaphore_wait(barrier, n - 1 + 2 * beside)

    def pass_token(up):
        @pl.when(lon > 0 if up else lon < ring - 1)
        def _():
            pl.semaphore_wait(token.at[int(up)], 1)

        toward(token.at[int(up)], up, 0)

    first, last = pl.ds(0, EDGE), pl.ds(top, EDGE)
    low, high = pl.ds(0, EDGE), pl.ds(EDGE + width, EDGE)
    held_first, held_last = pl.ds(EDGE, EDGE), pl.ds(EDGE + top, EDGE)
    inner, held_inner = pl.ds(EDGE, top - EDGE), pl.ds(2 * EDGE, top - EDGE)
    winds, humid = pl.ds(0, dyn), pl.ds(dyn, 1)
    slots = {"lo": 0, "hi": 1, "hum_lo": 2, "hum_hi": 3, "dyn": 4, "hum": 4 + half}

    def x_copy(q, t, kind, level=0):
        there = core_of(t) * half
        which = winds if kind in ("lo", "hi", "dyn") else humid
        if kind in ("dyn", "hum"):
            source = init_ref.at[0, which, there + level, inner]
            place = full.at[mem, which, level, held_inner]
        else:
            lower = kind in ("lo", "hum_lo")
            source = init_ref.at[0, which, pl.ds(there, half), first if lower else last]
            place = full.at[mem, which, :, held_first if lower else held_last]
        slot = slots[kind] + level
        return pltpu.make_async_remote_copy(
            src_ref=source,
            dst_ref=place,
            send_sem=x_send.at[2 * (q - 1) + t, slot],
            recv_sem=x_recv.at[2 * (q - 1) + t, slot],
            device_id={"mem": target(q, t)},
            device_id_type=MESH_ID,
        )

    def lon_copy(source, place, slot, side, t=0):
        return pltpu.make_async_remote_copy(
            src_ref=source,
            dst_ref=place,
            send_sem=z_send.at[slot, side],
            recv_sem=z_recv.at[slot, side],
            device_id={"lon": east if side else west, "mem": target(0, t)},
            device_id_type=MESH_ID,
        )

    def halo(t, side):
        return lon_copy(
            init_ref.at[0, :, pl.ds(core_of(t) * half, half), last if side else first],
            full.at[mem, :, :, low if side else high],
            t,
            side,
            t,
        )

    def kap_halo(side):
        return lon_copy(
            kap_ref.at[pl.ds(mine, half), last if side else first],
            kap.at[:, low if side else high],
            2,
            side,
        )

    def noise_copy(side):
        return lon_copy(noise_edge.at[side], noise_halo.at[1 - side], 3, side)

    def forward(q, t, kind, side):
        which = winds if kind == 0 else humid
        member = sender(q, t)
        slot = 2 * (2 * (q - 1) + t) + kind
        return pltpu.make_async_remote_copy(
            src_ref=full.at[member, which, :, held_last if side else held_first],
            dst_ref=full.at[member, which, :, low if side else high],
            send_sem=f_send.at[slot, side],
            recv_sem=f_recv.at[slot, side],
            device_id={"lon": east if side else west},
            device_id_type=MESH_ID,
        )

    def start_halo(near):
        for side, inside in enumerate((lon > 0, lon < ring - 1)):

            @pl.when(inside if near else jnp.logical_not(inside))
            def _():
                halo(0, side).start()
                halo(1, side).start()
                kap_halo(side).start()

    to_twin = [
        pltpu.make_async_remote_copy(
            src_ref=ids.at[core],
            dst_ref=ids.at[core],
            send_sem=p_send.at[0],
            recv_sem=p_recv.at[0],
            device_id={"mem": twin},
            device_id_type=MESH_ID,
        ),
        pltpu.make_async_remote_copy(
            src_ref=init_ref.at[0, :, pl.ds(half - mine, half)],
            dst_ref=full.at[mem, :, :, pl.ds(EDGE, width)],
            send_sem=p_send.at[1],
            recv_sem=p_recv.at[1],
            device_id={"mem": twin},
            device_id_type=MESH_ID,
        ),
    ]
    ahead = [("lo", 0), ("hi", 0)]
    behind = [("dyn", 0), ("hum_lo", 0), ("hum_hi", 0)]
    behind += [("dyn", level) for level in range(1, half)]
    behind += [("hum", level) for level in range(half)]
    pieces = ahead + behind
    for kind, level in ahead:
        for q, t in links:
            x_copy(q, t, kind, level).start()
    line = lax.broadcasted_iota(jnp.int32, (EDGE, lat), 0)
    ids[core] = jnp.where(line == 0, anc_ref[0], sel_ref[0])
    for copy in to_twin:
        copy.start()
    start_halo(True)
    for kind, level in behind:
        for q, t in links:
            x_copy(q, t, kind, level).start()

    @pl.when(2 * lon < ring)
    def _():
        pass_token(True)
        pass_token(False)

    @pl.when(2 * lon >= ring)
    def _():
        pass_token(False)
        pass_token(True)

    start_halo(False)

    local[3].wait()
    to_twin[0].wait_recv()
    kinds = pert.shape[0]
    packed = noise_edge.shape[3]
    clones = (core, 1 - core)

    def choose(level, carry):
        for k in range(2):
            chosen = ids[clones[k], 1:2, :]
            for f in range(fields):
                value = pert[0, f, level]
                for j in range(1, kinds):
                    value = jnp.where(chosen == j, pert[j, f, level], value)
                noise[k, f, level, EDGE : EDGE + width, :] = value
                blank = jnp.zeros((EDGE, lat), jnp.float32)
                noise[k, f, level, 0:EDGE, :] = blank
                noise[k, f, level, EDGE + width : rows, :] = blank
                spot = pl.ds(f * STEPS, STEPS)
                noise_edge[0, k, level, spot, :] = value[0:STEPS]
                noise_edge[1, k, level, spot, :] = value[width - STEPS : width]
            rest = packed - fields * STEPS
            if rest:
                for side in range(2):
                    noise_edge[side, k, level, pl.ds(fields * STEPS, rest), :] = jnp.zeros(
                        (rest, lat), jnp.float32
                    )
        return carry

    lax.fori_loop(0, half, choose, 0)
    for side in range(2):
        noise_copy(side).start()

    def pass_edges(kind):
        names = ("hum_lo", "hum_hi") if kind else ("lo", "hi")
        for q, t in links:
            for side in range(2):
                x_copy(q, t, names[side]).wait_recv()
                forward(q, t, kind, side).start()

    pass_edges(0)

    lane = lax.broadcasted_iota(jnp.int32, (rows, lat), 1)
    not_north = jnp.where(lane == lat - 1, 0.0, 1.0)
    not_south = jnp.where(lane == 0, 0.0, 1.0)

    def from_west(q):
        return pltpu.roll(q, 1, 0)

    def from_east(q):
        return pltpu.roll(q, rows - 1, 0)

    def from_south(q):
        return pltpu.roll(q, 1, 1)

    def from_north(q):
        return pltpu.roll(q, lat - 1, 1)

    def faces(level, carry):
        k = kap[level]
        to_east = (0.5 * TIME_STEP) * (k + from_east(k))
        to_north = (0.5 * TIME_STEP) * (k + from_north(k)) * not_north
        face[0, level] = to_east
        face[1, level] = from_west(to_east)
        face[2, level] = to_north
        face[3, level] = from_south(to_north)
        return carry

    def coefficients(u, v, level):
        u = TIME_STEP * u
        v = TIME_STEP * v
        to_e = face[0, level] - jnp.minimum(u, 0.0)
        to_w = face[1, level] + jnp.maximum(u, 0.0)
        to_n = face[2, level] - jnp.minimum(v, 0.0) * not_north
        to_s = face[3, level] + jnp.maximum(v, 0.0) * not_south
        here = 1.0 - ((to_e + to_w) + (to_n + to_s))
        return to_e, to_w, to_n, to_s, here

    def moved(q, c):
        to_e, to_w, to_n, to_s, here = c
        return (
            here * q
            + (to_e * from_east(q) + to_w * from_west(q))
            + (to_n * from_north(q) + to_s * from_south(q))
        )

    def observed(t):
        strip = t[EDGE : EDGE + width, :]
        terms = weight[...] * strip * strip
        return jnp.sum(terms.reshape(width // 8, 8, lat), axis=0)

    def advance(states, level, totals=None, keep=None):
        for step in range(STEPS):
            for k in range(len(states)):
                c = coefficients(states[k][0], states[k][1], level)
                if keep is not None:
                    held, rank = keep
                    for i in range(5):
                        held[rank + k, level, step, i] = c[i]
                states[k] = [moved(q, c) for q in states[k]]
                if totals is not None:
                    totals[k] = totals[k] + observed(states[k][2])
        return states, totals

    def glide(values, level, held, rank):
        for step in range(STEPS):
            for k in range(len(values)):
                values[k] = moved(values[k], [held[rank + k, level, step, i] for i in range(5)])
        return values

    for copy in local[:3]:
        copy.wait()
    for side in range(2):
        kap_halo(side).wait()
    lax.fori_loop(0, half, faces, 0)
    to_twin[1].wait_recv()
    for side in range(2):
        halo(0, side).wait()
        halo(1, side).wait()

    zero = jnp.zeros((8, lat), jnp.float32)
    own = (mem, twin)

    def own_level(level, totals):
        states = [[full[m, f, level] for f in range(fields)] for m in own]
        states, totals = advance(states, level, list(totals))
        for m, state in zip(own, states):
            for f in range(fields):
                mid[m, f, level] = state[f]
        return tuple(totals)

    totals = lax.fori_loop(0, half, own_level, (zero, zero))
    for k in range(2):
        acc[k, 0] = totals[k]

    for side in range(2):
        noise_copy(side).wait()

    def fringe(level, carry):
        for k in range(2):
            for f in range(fields):
                spot = slice(f * STEPS, (f + 1) * STEPS)
                noise[k, f, level, EDGE - STEPS : EDGE, :] = noise_halo[0, k, level, spot, :]
                noise[k, f, level, EDGE + width : EDGE + width + STEPS, :] = noise_halo[
                    1, k, level, spot, :
                ]
        return carry

    lax.fori_loop(0, half, fringe, 0)

    def cloned(k, f, level):
        ancestor = ids[clones[k], 0:1, :]
        value = mid[0, f, level]
        for j in range(1, n):
            value = jnp.where(ancestor == j, mid[j, f, level], value)
        return value + noise[k, f, level]

    def hand_over(kind, level):
        which = winds if kind == 0 else humid
        return pltpu.make_async_remote_copy(
            src_ref=stage.at[which, level],
            dst_ref=out_ref.at[0, which, mine + level],
            send_sem=o_send.at[kind, level],
            recv_sem=o_recv.at[kind, level],
            device_id={"mem": twin},
            device_id_type=MESH_ID,
        )

    strip = slice(EDGE, EDGE + width)
    for q, t in links:
        for side in range(2):
            forward(q, t, 0, side).wait_recv()

    def dyn_level(level, totals):
        for q in range(1, pairs):
            for t in range(2):
                x_copy(q, t, "dyn", level).wait_recv()
            group = [sender(q, t) for t in range(2)]
            states = [[full[m, f, level] for f in range(dyn)] for m in group]
            states, _ = advance(states, level, None, (coef_mid, 2 * (q - 1)))
            for m, state in zip(group, states):
                for f in range(dyn):
                    mid[m, f, level] = state[f]
        states = [[cloned(k, f, level) for f in range(dyn)] for k in range(2)]
        states, totals = advance(states, level, list(totals), (coef_end, 0))
        for f in range(dyn):
            out_ref[0, f, mine + level] = states[0][f][strip]
            stage[f, level] = states[1][f][strip]
        hand_over(0, level).start()

        @pl.when(level == 0)
        def _():
            pass_edges(1)

        return tuple(totals)

    totals = lax.fori_loop(0, half, dyn_level, (zero, zero))

    for k in range(2):
        acc[k, 1] = totals[k]
    part[lon, core] = acc[0]

    def share(d, t):
        return pltpu.make_async_remote_copy(
            src_ref=acc.at[t],
            dst_ref=part.at[lon, core],
            send_sem=s_send.at[d, t],
            recv_sem=s_recv.at[d, t],
            device_id={"lon": lax.rem(lon + d, ring), "mem": target(0, t)},
            device_id_type=MESH_ID,
        )

    shares = [share(d, t) for d in range(ring) for t in range(2) if (d, t) != (0, 0)]
    for copy in shares:
        copy.start()

    for q, t in links:
        for side in range(2):
            forward(q, t, 1, side).wait_recv()

    def hum_level(level, carry):
        for q in range(1, pairs):
            for t in range(2):
                x_copy(q, t, "hum", level).wait_recv()
            group = [sender(q, t) for t in range(2)]
            values = glide([full[m, dyn, level] for m in group], level, coef_mid, 2 * (q - 1))
            for m, value in zip(group, values):
                mid[m, dyn, level] = value
        values = glide([cloned(k, dyn, level) for k in range(2)], level, coef_end, 0)
        stage[dyn, level] = values[1][strip]
        hand_over(1, level).start()
        out_ref[0, dyn, mine + level] = values[0][strip]
        return carry

    lax.fori_loop(0, half, hum_level, 0)

    for copy in shares:
        copy.wait()
    cells = levels * lat * width * ring
    sums = jnp.sum(part[...].reshape(2 * ring, 2, 8, lat), axis=0)
    action = [jnp.sum(sums[which]) / cells for which in range(2)]
    column = lax.broadcasted_iota(jnp.int32, (1, 2), 1)
    act_ref[...] = jnp.where(column == 0, action[0], action[1])
    for kind, level in pieces:
        for q, t in links:
            x_copy(q, t, kind, level).wait_send()
    for q, t in links:
        for kind in range(2):
            for side in range(2):
                forward(q, t, kind, side).wait_send()
    for copy in to_twin:
        copy.wait_send()
    for level in range(half):
        for kind in range(2):
            hand_over(kind, level).wait()


def finish(state_ref, action_ref, state_out, action_out, sem):
    fields = state_ref.shape[1]
    copies = [
        pltpu.make_async_copy(state_ref.at[:, f], state_out.at[:, f], sem.at[f])
        for f in range(fields)
    ]
    copies.append(pltpu.make_async_copy(action_ref, action_out, sem.at[fields]))
    for copy in copies:
        copy.start()
    for copy in copies:
        copy.wait()


def body(initial_state, ancestor, selector, perturbations, diffusivity, region_weight):
    n, ring = lax.axis_size("mem"), lax.axis_size("lon")
    _, fields, levels, width, lat = initial_state.shape
    half = levels // 2
    rows = width + 2 * EDGE
    slots = 4 + 2 * half
    packed = -(-fields * STEPS // 8) * 8
    f32 = jnp.float32
    far = pl.BlockSpec(memory_space=pltpu.HBM)
    near = pl.BlockSpec(memory_space=pltpu.VMEM)
    scalar = pl.BlockSpec(memory_space=pltpu.SMEM)
    dma = pltpu.SemaphoreType.DMA
    state, action = pl.pallas_call(
        functools.partial(kernel, n, ring),
        out_shape=(pltpu.VMEM(initial_state.shape, f32), pltpu.VMEM((1, 2), f32)),
        in_specs=[scalar] * 2 + [far] * 4,
        out_specs=(near,) * 2,
        scratch_shapes=[
            pltpu.VMEM((n, fields, half, rows, lat), f32),
            pltpu.VMEM((n, fields, half, rows, lat), f32),
            pltpu.VMEM((2, fields, half, rows, lat), f32),
            pltpu.VMEM((perturbations.shape[0], fields, half, width, lat), f32),
            pltpu.VMEM((2, 2, half, packed, lat), f32),
            pltpu.VMEM((2, 2, half, packed, lat), f32),
            pltpu.VMEM((half, rows, lat), f32),
            pltpu.VMEM((4, half, rows, lat), f32),
            pltpu.VMEM((n - 2, half, STEPS, 5, rows, lat), f32),
            pltpu.VMEM((2, half, STEPS, 5, rows, lat), f32),
            pltpu.VMEM((width, lat), f32),
            pltpu.VMEM((fields, half, width, lat), f32),
            pltpu.VMEM((2, EDGE, lat), jnp.int32),
            pltpu.VMEM((2, 2, 8, lat), f32),
            pltpu.VMEM((ring, 2, 2, 8, lat), f32),
            dma((n - 2, slots)),
            dma((n - 2, slots)),
            dma((2,)),
            dma((2,)),
            dma((4, 2)),
            dma((4, 2)),
            dma((2 * (n - 2), 2)),
            dma((2 * (n - 2), 2)),
            dma((2, half)),
            dma((2, half)),
            dma((ring, 2)),
            dma((ring, 2)),
            dma((4,)),
            pltpu.SemaphoreType.REGULAR((2,)),
        ],
        compiler_params=pltpu.CompilerParams(
            collective_id=0, has_side_effects=True, vmem_limit_bytes=VMEM_LIMIT
        ),
    )(ancestor, selector, initial_state, perturbations, diffusivity, region_weight)
    return pl.pallas_call(
        finish,
        out_shape=(
            jax.ShapeDtypeStruct(initial_state.shape, f32),
            jax.ShapeDtypeStruct((1, 2), f32),
        ),
        in_specs=[near] * 2,
        out_specs=(far,) * 2,
        scratch_shapes=[dma((fields + 1,))],
        compiler_params=pltpu.CompilerParams(vmem_limit_bytes=1 << 20),
    )(state, action)


def solution(mesh):
    in_specs = (
        P(("ens", "mem"), None, None, "lon", None),
        P(("ens", "mem")),
        P(("ens", "mem")),
        P("ens", None, None, "lon", None),
        P(None, "lon", None),
        P("lon", None),
    )
    out_specs = (P(("ens", "mem"), None, None, "lon", None), P(("ens", "mem"), None))
    return jax.shard_map(body, mesh=mesh, in_specs=in_specs, out_specs=out_specs, check_vma=False)
```

```python
import functools

import jax
import jax.numpy as jnp
from jax import lax
from jax.experimental import pallas as pl
from jax.experimental.pallas import tpu as pltpu
from jax.sharding import PartitionSpec as P

STEPS = 3
TIME_STEP = 0.2
EDGE = 8
VMEM_LIMIT = 60000000
MESH_ID = pl.DeviceIdType.MESH


def kernel(
    n, ring, anc_ref, sel_ref, init_ref, pert_ref, kap_ref, weight_ref, res_ref, act_ref,
    state, halo_st, mid, mid_e, kap, kap_halo, face, face_e, pert, noise, pert_edge,
    pert_halo, stage, weight, ids, acc, block, spread, total, gather,
    i_send, i_recv, p_send, p_recv, z_send, z_recv, x_send, x_recv, g_send, g_recv,
    s_send, s_recv, local_sem, token,
):
    _, fields, levels, width, lat = init_ref.shape
    half = levels // 2
    pairs = n // 2
    top = width - EDGE
    outer = 6 * EDGE
    mem = lax.axis_index("mem")
    lon = lax.axis_index("lon")
    core = lax.rem(mem, 2)
    base = mem - core
    pair = mem // 2
    east, west = lax.rem(lon + 1, ring), lax.rem(lon + ring - 1, ring)
    mine = core * half
    relations = [(q, t) for q in range(pairs) for t in range(2)]

    def core_of(t):
        return core if t == 0 else 1 - core

    def target(q, t):
        return lax.rem(base + 2 * q, n) + core_of(t)

    local = [
        pltpu.make_async_copy(
            init_ref.at[0, :, pl.ds(mine, half)], state.at[core], local_sem.at[0]
        ),
        pltpu.make_async_copy(kap_ref.at[pl.ds(mine, half)], kap, local_sem.at[1]),
        pltpu.make_async_copy(weight_ref, weight, local_sem.at[2]),
        pltpu.make_async_copy(pert_ref.at[:, :, pl.ds(mine, half)], pert, local_sem.at[3]),
    ]

    barrier = pltpu.get_barrier_semaphore()
    for q, t in relations[1:]:
        pl.semaphore_signal(
            barrier, inc=1, device_id={"mem": target(q, t)}, device_id_type=MESH_ID
        )

    def toward(semaphore, up, t):
        @pl.when(lon < ring - 1 if up else lon > 0)
        def _():
            pl.semaphore_signal(
                semaphore,
                inc=1,
                device_id={"lon": east if up else west, "mem": target(0, t)},
                device_id_type=MESH_ID,
            )

    for t in range(2):
        toward(barrier, True, t)
        toward(barrier, False, t)
    for copy in local:
        copy.start()
    line = lax.broadcasted_iota(jnp.int32, (EDGE, lat), 0)
    ids[mem] = jnp.where(line == 0, anc_ref[0], sel_ref[0])
    beside = jnp.where(lon > 0, 1, 0) + jnp.where(lon < ring - 1, 1, 0)
    pl.semaphore_wait(barrier, n - 1 + 2 * beside)

    def pass_token(up):
        pl.semaphore_wait(token.at[int(up)], 1)
        toward(token.at[int(up)], up, 0)

    def send_ids(q, t):
        slot = 2 * q + t - 1
        return pltpu.make_async_remote_copy(
            src_ref=ids.at[mem],
            dst_ref=ids.at[mem],
            send_sem=i_send.at[slot],
            recv_sem=i_recv.at[slot],
            device_id={"mem": target(q, t)},
            device_id_type=MESH_ID,
        )

    to_twin = pltpu.make_async_remote_copy(
        src_ref=init_ref.at[0, :, pl.ds(half - mine, half)],
        dst_ref=state.at[core],
        send_sem=p_send,
        recv_sem=p_recv,
        device_id={"mem": target(0, 1)},
        device_id_type=MESH_ID,
    )

    def lon_copy(source, place, slot, side, t=0):
        return pltpu.make_async_remote_copy(
            src_ref=source,
            dst_ref=place,
            send_sem=z_send.at[slot, side],
            recv_sem=z_recv.at[slot, side],
            device_id={"lon": east if side else west, "mem": target(0, t)},
            device_id_type=MESH_ID,
        )

    def halo(t, side):
        rows = pl.ds(top if side else 0, EDGE)
        return lon_copy(
            init_ref.at[0, :, pl.ds(core_of(t) * half, half), rows],
            halo_st.at[core, 1 - side],
            t,
            side,
            t,
        )

    def kap_copy(side):
        rows = pl.ds(top if side else 0, EDGE)
        return lon_copy(kap_ref.at[pl.ds(mine, half), rows], kap_halo.at[1 - side], 2, side)

    def pert_copy(side):
        return lon_copy(pert_edge.at[side], pert_halo.at[1 - side], 3, side)

    def start_halo(side):
        halo(0, side).start()
        halo(1, side).start()
        kap_copy(side).start()

    for q, t in relations[1:]:
        send_ids(q, t).start()
    to_twin.start()
    for side, inside in enumerate((lon > 0, lon < ring - 1)):

        @pl.when(inside)
        def _():
            start_halo(side)

    @pl.when(lon == 0)
    def _():
        toward(token.at[1], True, 0)

    @pl.when(lon == ring - 1)
    def _():
        toward(token.at[0], False, 0)

    lane = lax.broadcasted_iota(jnp.int32, (width, lat), 1)
    not_north = jnp.where(lane == lat - 1, 0.0, 1.0)
    not_south = jnp.where(lane == 0, 0.0, 1.0)

    def from_west(q):
        return pltpu.roll(q, 1, 0)

    def from_east(q):
        return pltpu.roll(q, q.shape[0] - 1, 0)

    def from_south(q):
        return pltpu.roll(q, 1, 1)

    def from_north(q):
        return pltpu.roll(q, lat - 1, 1)

    def put_faces(held, level, k):
        to_east = (0.5 * TIME_STEP) * (k + from_east(k))
        to_north = (0.5 * TIME_STEP) * (k + from_north(k)) * not_north[: k.shape[0]]
        held[0, level] = to_east
        held[1, level] = from_west(to_east)
        held[2, level] = to_north
        held[3, level] = from_south(to_north)

    def coefficients(u, v, held, level):
        size = u.shape[0]
        u = TIME_STEP * u
        v = TIME_STEP * v
        to_e = held[0, level] - jnp.minimum(u, 0.0)
        to_w = held[1, level] + jnp.maximum(u, 0.0)
        to_n = held[2, level] - jnp.minimum(v, 0.0) * not_north[:size]
        to_s = held[3, level] + jnp.maximum(v, 0.0) * not_south[:size]
        here = 1.0 - ((to_e + to_w) + (to_n + to_s))
        return to_e, to_w, to_n, to_s, here

    def moved(q, c):
        to_e, to_w, to_n, to_s, here = c
        return (
            here * q
            + (to_e * from_east(q) + to_w * from_west(q))
            + (to_n * from_north(q) + to_s * from_south(q))
        )

    def observed(t):
        if t.shape[0] == width:
            strip, share = t[EDGE:top], weight[EDGE:top]
        else:
            strip = jnp.concatenate([t[EDGE : 2 * EDGE], t[4 * EDGE : 5 * EDGE]], axis=0)
            share = jnp.concatenate([weight[0:EDGE], weight[top:width]], axis=0)
        terms = share * strip * strip
        return jnp.sum(terms.reshape(-1, 8, lat), axis=0)

    def advance(states, held, spots, totals):
        for _ in range(STEPS):
            for k in range(len(states)):
                c = coefficients(states[k][0], states[k][1], held, spots[k])
                states[k] = [moved(q, c) for q in states[k]]
                totals[k] = totals[k] + observed(states[k][2])
        return states, totals

    zero = jnp.zeros((8, lat), jnp.float32)

    def inner_member(t):
        a = core_of(t)
        states = [[state[a, f, level] for f in range(fields)] for level in range(half)]
        states, totals = advance(states, face, list(range(half)), [zero] * half)
        for level in range(half):
            for f in range(fields):
                mid[a, f, level] = states[level][f]
        acc[t, 0] = functools.reduce(jnp.add, totals)

    for copy in local[:3]:
        copy.wait()
    for level in range(half):
        put_faces(face, level, kap[level])
    inner_member(0)

    kinds = pert.shape[0]
    packed = pert_edge.shape[3]
    local[3].wait()

    def pack(level, carry):
        for j in range(kinds):
            for f in range(fields):
                spot = pl.ds(f * STEPS, STEPS)
                pert_edge[0, j, level, spot, :] = pert[j, f, level, 0:STEPS, :]
                pert_edge[1, j, level, spot, :] = pert[j, f, level, width - STEPS : width, :]
            rest = packed - fields * STEPS
            if rest:
                for side in range(2):
                    pert_edge[side, j, level, pl.ds(fields * STEPS, rest), :] = jnp.zeros(
                        (rest, lat), jnp.float32
                    )
        return carry

    lax.fori_loop(0, half, pack, 0)
    for side, inside in enumerate((lon > 0, lon < ring - 1)):

        @pl.when(inside)
        def _():
            pert_copy(side).start()

    @pl.when(2 * lon >= ring)
    def _():
        @pl.when(lon < ring - 1)
        def _():
            pass_token(False)

        pass_token(True)

        @pl.when(lon == ring - 1)
        def _():
            start_halo(1)
            pert_copy(1).start()

    to_twin.wait_recv()
    inner_member(1)

    @pl.when(jnp.logical_and(lon > 0, 2 * lon < ring))
    def _():
        pass_token(True)
        pass_token(False)

    for q, t in relations[1:]:
        send_ids(q, t).wait_recv()

    def choose(q, level):
        for t in range(2):
            chosen = ids[target(q, t), 1:2, :]
            for f in range(fields):
                value = pert[0, f, level]
                for j in range(1, kinds):
                    value = jnp.where(chosen == j, pert[j, f, level], value)
                noise[2 * q + t, f, level] = value

    def result(q, t, piece):
        r = 2 * q + t
        if piece is None or not isinstance(piece, str):
            place = (piece, pl.ds(EDGE, top - EDGE))
            there = (mine + piece, pl.ds(EDGE, top - EDGE))
            slot = piece
        else:
            rows = pl.ds(0 if piece == "lo" else top, EDGE)
            place = (pl.ds(0, half), rows)
            there = (pl.ds(mine, half), rows)
            slot = half + int(piece == "hi")
        return pltpu.make_async_remote_copy(
            src_ref=stage.at[r, :, place[0], place[1]],
            dst_ref=res_ref.at[pair, :, there[0], there[1]],
            send_sem=x_send.at[r - 1, slot],
            recv_sem=x_recv.at[r - 1, slot],
            device_id={"mem": target(q, t)},
            device_id_type=MESH_ID,
        )

    def put(q, t, f, level, rows, value):
        if (q, t) == (0, 0):
            res_ref[pair, f, mine + level, rows, :] = value
        else:
            stage[2 * q + t, f, level, rows, :] = value

    def second(q, t):
        return ids[target(q, t), 0:1, :] == base + 1

    def inner_clones(q):
        def one(level, totals):
            choose(q, level)
            states = [
                [
                    jnp.where(second(q, t), mid[1, f, level], mid[0, f, level])
                    + noise[2 * q + t, f, level]
                    for f in range(fields)
                ]
                for t in range(2)
            ]
            states, totals = advance(states, face, [level] * 2, list(totals))
            for t in range(2):
                for f in range(fields):
                    put(q, t, f, level, slice(EDGE, top), states[t][f][EDGE:top])
                if (q, t) != (0, 0):
                    result(q, t, level).start()
            return tuple(totals)

        totals = lax.fori_loop(0, half, one, (zero, zero))
        for t in range(2):
            acc[2 * q + t, 1] = totals[t]

    for q in range(1, pairs):
        inner_clones(q)

    @pl.when(lon == 0)
    def _():
        pl.semaphore_wait(token.at[0], 1)
        start_halo(0)
        pert_copy(0).start()

    inner_clones(0)

    for side in range(2):
        kap_copy(side).wait()
        halo(0, side).wait()
        halo(1, side).wait()

    def framed(before, middle, after):
        return jnp.concatenate(
            [before, middle[0 : 2 * EDGE], middle[width - 2 * EDGE : width], after], axis=0
        )

    def outer_members(level, totals):
        put_faces(face_e, level, framed(kap_halo[0, level], kap[level], kap_halo[1, level]))
        states = [
            [
                framed(halo_st[a, 0, f, level], state[a, f, level], halo_st[a, 1, f, level])
                for f in range(fields)
            ]
            for a in (core, 1 - core)
        ]
        states, totals = advance(states, face_e, [level] * 2, list(totals))
        for t in range(2):
            for f in range(fields):
                mid_e[core_of(t), f, level] = states[t][f]
        return tuple(totals)

    totals = lax.fori_loop(0, half, outer_members, (zero, zero))
    for t in range(2):
        acc[t, 0] = acc[t, 0] + totals[t]
    for side in range(2):
        pert_copy(side).wait()

    def outer_clones(q):
        def one(level, totals):
            states = []
            blank = jnp.zeros((EDGE - STEPS, lat), jnp.float32)
            for t in range(2):
                r = 2 * q + t
                chosen = ids[target(q, t), 1:2, :]
                ends = []
                for side in range(2):
                    value = pert_halo[side, 0, level]
                    for j in range(1, kinds):
                        value = jnp.where(chosen == j, pert_halo[side, j, level], value)
                    ends.append(value)
                fresh = []
                for f in range(fields):
                    spot = slice(f * STEPS, (f + 1) * STEPS)
                    before = jnp.concatenate([blank, ends[0][spot]], axis=0)
                    after = jnp.concatenate([ends[1][spot], blank], axis=0)
                    fresh.append(
                        jnp.where(second(q, t), mid_e[1, f, level], mid_e[0, f, level])
                        + framed(before, noise[r, f, level], after)
                    )
                states.append(fresh)
            states, totals = advance(states, face_e, [level] * 2, list(totals))
            for t in range(2):
                for f in range(fields):
                    put(q, t, f, level, slice(0, EDGE), states[t][f][EDGE : 2 * EDGE])
                    put(q, t, f, level, slice(top, width), states[t][f][4 * EDGE : 5 * EDGE])
            return tuple(totals)

        totals = lax.fori_loop(0, half, one, (zero, zero))
        for t in range(2):
            if (q, t) != (0, 0):
                result(q, t, "lo").start()
                result(q, t, "hi").start()
            r = 2 * q + t
            ancestor = ids[target(q, t), 0:1, :]
            held = jnp.logical_or(ancestor == base, ancestor == base + 1)
            acc[r, 1] = jnp.where(held, acc[r, 1] + totals[t], 0.0)
            if q:
                acc[r, 0] = zero

    for q in range(1, pairs):
        outer_clones(q)
    outer_clones(0)

    block[...] = jnp.concatenate(
        [
            jnp.sum(acc[2 * q + t, which], axis=0, keepdims=True)
            for q, t in relations
            for which in range(2)
        ],
        axis=0,
    )
    spread[lon] = block[...]
    shares = [
        pltpu.make_async_remote_copy(
            src_ref=block,
            dst_ref=spread.at[lon],
            send_sem=s_send.at[d - 1],
            recv_sem=s_recv.at[d - 1],
            device_id={"lon": lax.rem(lon + d, ring)},
            device_id_type=MESH_ID,
        )
        for d in range(1, ring)
    ]
    for copy in shares:
        copy.start()
    for copy in shares:
        copy.wait_recv()

    def hand(q, t):
        r = 2 * q + t
        return pltpu.make_async_remote_copy(
            src_ref=total,
            dst_ref=gather.at[r],
            send_sem=g_send.at[r - 1],
            recv_sem=g_recv.at[r - 1],
            device_id={"mem": target(q, t)},
            device_id_type=MESH_ID,
        )

    whole = jnp.sum(spread[...], axis=0)
    total[...] = whole
    gather[0] = whole
    for q, t in relations[1:]:
        hand(q, t).start()
    for q, t in relations[1:]:
        hand(q, t).wait_recv()
    cells = levels * lat * width * ring
    action = []
    for which in range(2):
        rows = [gather[r, 2 * r + which : 2 * r + which + 1, :] for r in range(n)]
        action.append(jnp.sum(functools.reduce(jnp.add, rows)) / cells)
    column = lax.broadcasted_iota(jnp.int32, (1, 2), 1)
    act_ref[...] = jnp.where(column == 0, action[0], action[1])

    for copy in shares:
        copy.wait_send()
    for q, t in relations[1:]:
        hand(q, t).wait_send()
    for q, t in relations[1:]:
        send_ids(q, t).wait_send()
    to_twin.wait_send()
    for piece in list(range(half)) + ["lo", "hi"]:
        for q, t in relations[1:]:
            result(q, t, piece).wait()


def finish(anc_ref, res_ref, action_ref, state_out, action_out, sem):
    fields = res_ref.shape[1]
    chosen = anc_ref[0] // 2
    copies = [
        pltpu.make_async_copy(res_ref.at[chosen, f], state_out.at[0, f], sem.at[f])
        for f in range(fields)
    ]
    copies.append(pltpu.make_async_copy(action_ref, action_out, sem.at[fields]))
    for copy in copies:
        copy.start()
    for copy in copies:
        copy.wait()


def body(initial_state, ancestor, selector, perturbations, diffusivity, region_weight):
    n, ring = lax.axis_size("mem"), lax.axis_size("lon")
    _, fields, levels, width, lat = initial_state.shape
    half, pairs = levels // 2, n // 2
    kinds = perturbations.shape[0]
    outer = 6 * EDGE
    packed = -(-fields * STEPS // 8) * 8
    f32 = jnp.float32
    far = pl.BlockSpec(memory_space=pltpu.HBM)
    near = pl.BlockSpec(memory_space=pltpu.VMEM)
    scalar = pl.BlockSpec(memory_space=pltpu.SMEM)
    dma = pltpu.SemaphoreType.DMA
    results, action = pl.pallas_call(
        functools.partial(kernel, n, ring),
        out_shape=(
            pltpu.VMEM((pairs, fields, levels, width, lat), f32),
            pltpu.VMEM((1, 2), f32),
        ),
        in_specs=[scalar] * 2 + [far] * 4,
        out_specs=(near,) * 2,
        scratch_shapes=[
            pltpu.VMEM((2, fields, half, width, lat), f32),
            pltpu.VMEM((2, 2, fields, half, EDGE, lat), f32),
            pltpu.VMEM((2, fields, half, width, lat), f32),
            pltpu.VMEM((2, fields, half, outer, lat), f32),
            pltpu.VMEM((half, width, lat), f32),
            pltpu.VMEM((2, half, EDGE, lat), f32),
            pltpu.VMEM((4, half, width, lat), f32),
            pltpu.VMEM((4, half, outer, lat), f32),
            pltpu.VMEM((kinds, fields, half, width, lat), f32),
            pltpu.VMEM((n, fields, half, width, lat), f32),
            pltpu.VMEM((2, kinds, half, packed, lat), f32),
            pltpu.VMEM((2, kinds, half, packed, lat), f32),
            pltpu.VMEM((n, fields, half, width, lat), f32),
            pltpu.VMEM((width, lat), f32),
            pltpu.VMEM((n, EDGE, lat), jnp.int32),
            pltpu.VMEM((n, 2, 8, lat), f32),
            pltpu.VMEM((2 * n, lat), f32),
            pltpu.VMEM((ring, 2 * n, lat), f32),
            pltpu.VMEM((2 * n, lat), f32),
            pltpu.VMEM((n, 2 * n, lat), f32),
            dma((n - 1,)),
            dma((n - 1,)),
            dma,
            dma,
            dma((4, 2)),
            dma((4, 2)),
            dma((n - 1, half + 2)),
            dma((n - 1, half + 2)),
            dma((n - 1,)),
            dma((n - 1,)),
            dma((ring - 1,)),
            dma((ring - 1,)),
            dma((4,)),
            pltpu.SemaphoreType.REGULAR((2,)),
        ],
        compiler_params=pltpu.CompilerParams(
            collective_id=0, has_side_effects=True, vmem_limit_bytes=VMEM_LIMIT
        ),
    )(ancestor, selector, initial_state, perturbations, diffusivity, region_weight)
    return pl.pallas_call(
        finish,
        out_shape=(
            jax.ShapeDtypeStruct(initial_state.shape, f32),
            jax.ShapeDtypeStruct((1, 2), f32),
        ),
        in_specs=[scalar, near, near],
        out_specs=(far,) * 2,
        scratch_shapes=[dma((fields + 1,))],
        compiler_params=pltpu.CompilerParams(vmem_limit_bytes=1 << 20),
    )(ancestor, results, action)


def solution(mesh):
    in_specs = (
        P(("ens", "mem"), None, None, "lon", None),
        P(("ens", "mem")),
        P(("ens", "mem")),
        P("ens", None, None, "lon", None),
        P(None, "lon", None),
        P("lon", None),
    )
    out_specs = (P(("ens", "mem"), None, None, "lon", None), P(("ens", "mem"), None))
    return jax.shard_map(body, mesh=mesh, in_specs=in_specs, out_specs=out_specs, check_vma=False)
```

```python
import functools

import jax
import jax.numpy as jnp
from jax import lax
from jax.experimental import pallas as pl
from jax.experimental.pallas import tpu as pltpu
from jax.sharding import PartitionSpec as P

STEPS = 3
TIME_STEP = 0.2
EDGE = 8
VMEM_LIMIT = 60000000
MESH_ID = pl.DeviceIdType.MESH


def kernel(
    n, ring, anc_ref, sel_ref, init_ref, pert_ref, kap_ref, weight_ref, res_ref, act_ref,
    state, frame, mid, mid_e, kap, kap_frame, face, face_e, pert, noise, noise_e,
    pert_edge, pert_halo, stage, weight, ids, acc, block, spread, total, gather,
    i_send, i_recv, p_send, p_recv, z_send, z_recv, x_send, x_recv, g_send, g_recv,
    s_send, s_recv, local_sem, token,
):
    _, fields, levels, width, lat = init_ref.shape
    half = levels // 2
    pairs = n // 2
    top = width - EDGE
    outer = 3 * EDGE
    mem = lax.axis_index("mem")
    lon = lax.axis_index("lon")
    core = lax.rem(mem, 2)
    base = mem - core
    pair = mem // 2
    east, west = lax.rem(lon + 1, ring), lax.rem(lon + ring - 1, ring)
    mine = core * half
    relations = [(q, t) for q in range(pairs) for t in range(2)]

    def core_of(t):
        return core if t == 0 else 1 - core

    def target(q, t):
        return lax.rem(base + 2 * q, n) + core_of(t)

    local = [
        pltpu.make_async_copy(
            init_ref.at[0, :, pl.ds(mine, half)], state.at[core], local_sem.at[0]
        ),
        pltpu.make_async_copy(kap_ref.at[pl.ds(mine, half)], kap, local_sem.at[1]),
        pltpu.make_async_copy(weight_ref, weight, local_sem.at[2]),
        pltpu.make_async_copy(pert_ref.at[:, :, pl.ds(mine, half)], pert, local_sem.at[3]),
    ]

    barrier = pltpu.get_barrier_semaphore()
    for q, t in relations[1:]:
        pl.semaphore_signal(
            barrier, inc=1, device_id={"mem": target(q, t)}, device_id_type=MESH_ID
        )

    def toward(semaphore, up, t):
        @pl.when(lon < ring - 1 if up else lon > 0)
        def _():
            pl.semaphore_signal(
                semaphore,
                inc=1,
                device_id={"lon": east if up else west, "mem": target(0, t)},
                device_id_type=MESH_ID,
            )

    for t in range(2):
        toward(barrier, True, t)
        toward(barrier, False, t)
    for copy in local:
        copy.start()
    line = lax.broadcasted_iota(jnp.int32, (EDGE, lat), 0)
    ids[mem] = jnp.where(line == 0, anc_ref[0], sel_ref[0])
    beside = jnp.where(lon > 0, 1, 0) + jnp.where(lon < ring - 1, 1, 0)
    pl.semaphore_wait(barrier, n - 1 + 2 * beside)

    def pass_token(up):
        pl.semaphore_wait(token.at[int(up)], 1)
        toward(token.at[int(up)], up, 0)

    def send_ids(q, t):
        slot = 2 * q + t - 1
        return pltpu.make_async_remote_copy(
            src_ref=ids.at[mem],
            dst_ref=ids.at[mem],
            send_sem=i_send.at[slot],
            recv_sem=i_recv.at[slot],
            device_id={"mem": target(q, t)},
            device_id_type=MESH_ID,
        )

    to_twin = pltpu.make_async_remote_copy(
        src_ref=init_ref.at[0, :, pl.ds(half - mine, half)],
        dst_ref=state.at[core],
        send_sem=p_send,
        recv_sem=p_recv,
        device_id={"mem": target(0, 1)},
        device_id_type=MESH_ID,
    )

    def lon_copy(source, place, slot, side, t=0):
        return pltpu.make_async_remote_copy(
            src_ref=source,
            dst_ref=place,
            send_sem=z_send.at[slot, side],
            recv_sem=z_recv.at[slot, side],
            device_id={"lon": jnp.where(side == 1, east, west), "mem": target(0, t)},
            device_id_type=MESH_ID,
        )

    def edge_rows(w):
        return pl.ds(pl.multiple_of(top * w, EDGE), EDGE)

    def beyond(w):
        return pl.ds(pl.multiple_of(2 * EDGE * w, EDGE), EDGE)

    def halo(t, side):
        return lon_copy(
            init_ref.at[0, :, pl.ds(core_of(t) * half, half), edge_rows(side)],
            frame.at[1 - side, core, :, :, beyond(1 - side)],
            t,
            side,
            t,
        )

    def kap_copy(side):
        return lon_copy(
            kap_ref.at[pl.ds(mine, half), edge_rows(side)],
            kap_frame.at[1 - side, :, beyond(1 - side)],
            2,
            side,
        )

    def pert_copy(side):
        return lon_copy(pert_edge.at[side], pert_halo.at[1 - side], 3, side)

    def start_halo(side):
        halo(0, side).start()
        halo(1, side).start()
        kap_copy(side).start()

    for q, t in relations[1:]:
        send_ids(q, t).start()
    to_twin.start()
    for side, inside in enumerate((lon > 0, lon < ring - 1)):

        @pl.when(inside)
        def _():
            start_halo(side)

    @pl.when(lon == 0)
    def _():
        toward(token.at[1], True, 0)

    @pl.when(lon == ring - 1)
    def _():
        toward(token.at[0], False, 0)

    lower = jnp.logical_and(lon > 0, 2 * lon < ring)

    @pl.when(lower)
    def _():
        pass_token(True)

    lane = lax.broadcasted_iota(jnp.int32, (width, lat), 1)
    not_north = jnp.where(lane == lat - 1, 0.0, 1.0)
    not_south = jnp.where(lane == 0, 0.0, 1.0)

    def from_west(q):
        return pltpu.roll(q, 1, 0)

    def from_east(q):
        return pltpu.roll(q, q.shape[0] - 1, 0)

    def from_south(q):
        return pltpu.roll(q, 1, 1)

    def from_north(q):
        return pltpu.roll(q, lat - 1, 1)

    def put_faces(held, level, k):
        to_east = (0.5 * TIME_STEP) * (k + from_east(k))
        to_north = (0.5 * TIME_STEP) * (k + from_north(k)) * not_north[: k.shape[0]]
        held[0, level] = to_east
        held[1, level] = from_west(to_east)
        held[2, level] = to_north
        held[3, level] = from_south(to_north)

    def coefficients(u, v, held, level):
        size = u.shape[0]
        u = TIME_STEP * u
        v = TIME_STEP * v
        to_e = held[0, level] - jnp.minimum(u, 0.0)
        to_w = held[1, level] + jnp.maximum(u, 0.0)
        to_n = held[2, level] - jnp.minimum(v, 0.0) * not_north[:size]
        to_s = held[3, level] + jnp.maximum(v, 0.0) * not_south[:size]
        here = 1.0 - ((to_e + to_w) + (to_n + to_s))
        return to_e, to_w, to_n, to_s, here

    def moved(q, c):
        to_e, to_w, to_n, to_s, here = c
        return (
            here * q
            + (to_e * from_east(q) + to_w * from_west(q))
            + (to_n * from_north(q) + to_s * from_south(q))
        )

    def observed(t, share):
        terms = share * t * t
        return jnp.sum(terms.reshape(-1, 8, lat), axis=0)

    def look_inner(t):
        return observed(t[EDGE:top], weight[EDGE:top])

    def advance(states, held, spots, totals, look):
        for _ in range(STEPS):
            for k in range(len(states)):
                c = coefficients(states[k][0], states[k][1], held, spots[k])
                states[k] = [moved(q, c) for q in states[k]]
                totals[k] = totals[k] + look(states[k][2])
        return states, totals

    zero = jnp.zeros((8, lat), jnp.float32)

    def inner_member(t):
        a = core_of(t)
        states = [[state[a, f, level] for f in range(fields)] for level in range(half)]
        states, totals = advance(states, face, list(range(half)), [zero] * half, look_inner)
        for level in range(half):
            for f in range(fields):
                mid[a, f, level] = states[level][f]
        acc[t, 0] = functools.reduce(jnp.add, totals)

    for copy in local[:3]:
        copy.wait()
    for level in range(half):
        put_faces(face, level, kap[level])
    inner_member(0)

    kinds = pert.shape[0]
    packed = pert_edge.shape[2]
    used = half * fields * STEPS
    local[3].wait()

    def pack(j, carry):
        for level in range(half):
            for f in range(fields):
                spot = pl.ds((level * fields + f) * STEPS, STEPS)
                pert_edge[0, j, spot, :] = pert[j, f, level, 0:STEPS, :]
                pert_edge[1, j, spot, :] = pert[j, f, level, width - STEPS : width, :]
        if packed > used:
            for side in range(2):
                pert_edge[side, j, pl.ds(used, packed - used), :] = jnp.zeros(
                    (packed - used, lat), jnp.float32
                )
        return carry

    lax.fori_loop(0, kinds, pack, 0)
    for side, inside in enumerate((lon > 0, lon < ring - 1)):

        @pl.when(inside)
        def _():
            pert_copy(side).start()

    @pl.when(2 * lon >= ring)
    def _():
        pass_token(True)

        @pl.when(lon < ring - 1)
        def _():
            pass_token(False)

        @pl.when(lon == ring - 1)
        def _():
            start_halo(1)
            pert_copy(1).start()

    to_twin.wait_recv()
    inner_member(1)

    @pl.when(lower)
    def _():
        pass_token(False)

    for q, t in relations[1:]:
        send_ids(q, t).wait_recv()

    def choose(q, t, level):
        chosen = ids[target(q, t), 1:2, :]
        for f in range(fields):
            value = pert[0, f, level]
            for j in range(1, kinds):
                value = jnp.where(chosen == j, pert[j, f, level], value)
            noise[2 * q + t, f, level] = value

    def piece(q, t, slot, levels_here, levels_there, rows):
        r = 2 * q + t
        return pltpu.make_async_remote_copy(
            src_ref=stage.at[r, :, levels_here, rows],
            dst_ref=res_ref.at[pair, :, levels_there, rows],
            send_sem=x_send.at[r - 1, slot],
            recv_sem=x_recv.at[r - 1, slot],
            device_id={"mem": target(q, t)},
            device_id_type=MESH_ID,
        )

    def inner_piece(q, t, level):
        return piece(q, t, level, level, mine + level, pl.ds(EDGE, top - EDGE))

    def outer_piece(q, t, w):
        return piece(q, t, half + w, pl.ds(0, half), pl.ds(mine, half), edge_rows(w))

    def put(q, t, f, level, rows, value):
        if (q, t) == (0, 0):
            res_ref[pair, f, mine + level, rows, :] = value
        else:
            stage[2 * q + t, f, level, rows, :] = value

    def second(q, t):
        return ids[target(q, t), 0:1, :] == base + 1

    def inner_clones(q):
        def one(level, totals):
            totals = list(totals)
            for t in range(2):
                choose(q, t, level)
                states = [
                    [
                        jnp.where(second(q, t), mid[1, f, level], mid[0, f, level])
                        + noise[2 * q + t, f, level]
                        for f in range(fields)
                    ]
                ]
                states, (totals[t],) = advance(states, face, [level], [totals[t]], look_inner)
                for f in range(fields):
                    put(q, t, f, level, slice(EDGE, top), states[0][f][EDGE:top])
                if (q, t) != (0, 0):
                    inner_piece(q, t, level).start()
            return tuple(totals)

        totals = lax.fori_loop(0, half, one, (zero, zero))
        for t in range(2):
            acc[2 * q + t, 1] = totals[t]

    for q in range(1, pairs):
        inner_clones(q)

    @pl.when(lon == 0)
    def _():
        pl.semaphore_wait(token.at[0], 1)
        start_halo(0)
        pert_copy(0).start()

    inner_clones(0)

    blank = jnp.zeros((EDGE - STEPS, lat), jnp.float32)

    def outer_rows(turn, carry):
        w = jnp.where(lon == 0, 1 - turn, turn)
        here = pl.ds(pl.multiple_of(EDGE * (1 - w), EDGE), 2 * EDGE)
        there = pl.ds(pl.multiple_of((width - 2 * EDGE) * w, EDGE), 2 * EDGE)

        def look_outer(t):
            return observed(t[EDGE : 2 * EDGE], weight[edge_rows(w)])

        kap_copy(1 - w).wait_recv()
        halo(0, 1 - w).wait_recv()
        halo(1, 1 - w).wait_recv()

        spots = [(level, t) for level in range(half) for t in range(2)]
        states = []
        for level in range(half):
            kap_frame[w, level, here, :] = kap[level, there, :]
            put_faces(face_e, level, kap_frame[w, level])
        for level, t in spots:
            for f in range(fields):
                frame[w, core_of(t), f, level, here, :] = state[core_of(t), f, level, there, :]
            states.append([frame[w, core_of(t), f, level] for f in range(fields)])
        grounds = [level for level, _ in spots]
        states, totals = advance(states, face_e, grounds, [zero] * len(spots), look_outer)
        for (level, t), fresh, total_of in zip(spots, states, totals):
            for f in range(fields):
                mid_e[core_of(t), f, level] = fresh[f]
            acc[t, 0] = acc[t, 0] + total_of
        pert_copy(1 - w).wait_recv()

        for q in list(range(1, pairs)) + [0]:

            states = []
            for level, t in spots:
                r = 2 * q + t
                chosen = ids[target(q, t), 1:2, :]
                ends = pert_halo[w, 0]
                for j in range(1, kinds):
                    ends = jnp.where(chosen == j, pert_halo[w, j], ends)
                fresh = []
                for f in range(fields):
                    start = (level * fields + f) * STEPS
                    rim = ends[start : start + STEPS]
                    noise_e[level, t, f, here, :] = noise[r, f, level, there, :]
                    noise_e[level, t, f, beyond(w), :] = jnp.where(
                        w == 0,
                        jnp.concatenate([blank, rim], axis=0),
                        jnp.concatenate([rim, blank], axis=0),
                    )
                    fresh.append(
                        jnp.where(second(q, t), mid_e[1, f, level], mid_e[0, f, level])
                        + noise_e[level, t, f]
                    )
                states.append(fresh)
            states, totals = advance(states, face_e, grounds, [zero] * len(spots), look_outer)
            for (level, t), fresh, total_of in zip(spots, states, totals):
                for f in range(fields):
                    put(q, t, f, level, edge_rows(w), fresh[f][EDGE : 2 * EDGE])
                acc[2 * q + t, 1] = acc[2 * q + t, 1] + total_of
            for t in range(2):
                if (q, t) != (0, 0):
                    outer_piece(q, t, w).start()
        return carry

    lax.fori_loop(0, 2, outer_rows, 0)
    for q, t in relations:
        r = 2 * q + t
        ancestor = ids[target(q, t), 0:1, :]
        held = jnp.logical_or(ancestor == base, ancestor == base + 1)
        acc[r, 1] = jnp.where(held, acc[r, 1], 0.0)
        if q:
            acc[r, 0] = zero

    block[...] = jnp.concatenate(
        [
            jnp.sum(acc[2 * q + t, which], axis=0, keepdims=True)
            for q, t in relations
            for which in range(2)
        ],
        axis=0,
    )
    spread[lon] = block[...]
    shares = [
        pltpu.make_async_remote_copy(
            src_ref=block,
            dst_ref=spread.at[lon],
            send_sem=s_send.at[d - 1],
            recv_sem=s_recv.at[d - 1],
            device_id={"lon": lax.rem(lon + d, ring)},
            device_id_type=MESH_ID,
        )
        for d in range(1, ring)
    ]
    for copy in shares:
        copy.start()
    for copy in shares:
        copy.wait_recv()

    def hand(q, t):
        r = 2 * q + t
        return pltpu.make_async_remote_copy(
            src_ref=total,
            dst_ref=gather.at[r],
            send_sem=g_send.at[r - 1],
            recv_sem=g_recv.at[r - 1],
            device_id={"mem": target(q, t)},
            device_id_type=MESH_ID,
        )

    whole = jnp.sum(spread[...], axis=0)
    total[...] = whole
    gather[0] = whole
    for q, t in relations[1:]:
        hand(q, t).start()
    for q, t in relations[1:]:
        hand(q, t).wait_recv()
    cells = levels * lat * width * ring
    action = []
    for which in range(2):
        rows = [gather[r, 2 * r + which : 2 * r + which + 1, :] for r in range(n)]
        action.append(jnp.sum(functools.reduce(jnp.add, rows)) / cells)
    column = lax.broadcasted_iota(jnp.int32, (1, 2), 1)
    act_ref[...] = jnp.where(column == 0, action[0], action[1])

    for copy in shares:
        copy.wait_send()
    for q, t in relations[1:]:
        hand(q, t).wait_send()
    for q, t in relations[1:]:
        send_ids(q, t).wait_send()
    to_twin.wait_send()
    for side in range(2):
        kap_copy(side).wait_send()
        pert_copy(side).wait_send()
        for t in range(2):
            halo(t, side).wait_send()
    for q, t in relations[1:]:
        for level in range(half):
            inner_piece(q, t, level).wait()
        for w in range(2):
            outer_piece(q, t, w).wait()


def finish(anc_ref, res_ref, action_ref, state_out, action_out, sem):
    fields = res_ref.shape[1]
    chosen = anc_ref[0] // 2
    copies = [
        pltpu.make_async_copy(res_ref.at[chosen, f], state_out.at[0, f], sem.at[f])
        for f in range(fields)
    ]
    copies.append(pltpu.make_async_copy(action_ref, action_out, sem.at[fields]))
    for copy in copies:
        copy.start()
    for copy in copies:
        copy.wait()


def body(initial_state, ancestor, selector, perturbations, diffusivity, region_weight):
    n, ring = lax.axis_size("mem"), lax.axis_size("lon")
    _, fields, levels, width, lat = initial_state.shape
    half, pairs = levels // 2, n // 2
    kinds = perturbations.shape[0]
    outer = 3 * EDGE
    packed = -(-half * fields * STEPS // 8) * 8
    f32 = jnp.float32
    far = pl.BlockSpec(memory_space=pltpu.HBM)
    near = pl.BlockSpec(memory_space=pltpu.VMEM)
    scalar = pl.BlockSpec(memory_space=pltpu.SMEM)
    dma = pltpu.SemaphoreType.DMA
    results, action = pl.pallas_call(
        functools.partial(kernel, n, ring),
        out_shape=(
            pltpu.VMEM((pairs, fields, levels, width, lat), f32),
            pltpu.VMEM((1, 2), f32),
        ),
        in_specs=[scalar] * 2 + [far] * 4,
        out_specs=(near,) * 2,
        scratch_shapes=[
            pltpu.VMEM((2, fields, half, width, lat), f32),
            pltpu.VMEM((2, 2, fields, half, outer, lat), f32),
            pltpu.VMEM((2, fields, half, width, lat), f32),
            pltpu.VMEM((2, fields, half, outer, lat), f32),
            pltpu.VMEM((half, width, lat), f32),
            pltpu.VMEM((2, half, outer, lat), f32),
            pltpu.VMEM((4, half, width, lat), f32),
            pltpu.VMEM((4, half, outer, lat), f32),
            pltpu.VMEM((kinds, fields, half, width, lat), f32),
            pltpu.VMEM((n, fields, half, width, lat), f32),
            pltpu.VMEM((half, 2, fields, outer, lat), f32),
            pltpu.VMEM((2, kinds, packed, lat), f32),
            pltpu.VMEM((2, kinds, packed, lat), f32),
            pltpu.VMEM((n, fields, half, width, lat), f32),
            pltpu.VMEM((width, lat), f32),
            pltpu.VMEM((n, EDGE, lat), jnp.int32),
            pltpu.VMEM((n, 2, 8, lat), f32),
            pltpu.VMEM((2 * n, lat), f32),
            pltpu.VMEM((ring, 2 * n, lat), f32),
            pltpu.VMEM((2 * n, lat), f32),
            pltpu.VMEM((n, 2 * n, lat), f32),
            dma((n - 1,)),
            dma((n - 1,)),
            dma,
            dma,
            dma((4, 2)),
            dma((4, 2)),
            dma((n - 1, half + 2)),
            dma((n - 1, half + 2)),
            dma((n - 1,)),
            dma((n - 1,)),
            dma((ring - 1,)),
            dma((ring - 1,)),
            dma((4,)),
            pltpu.SemaphoreType.REGULAR((2,)),
        ],
        compiler_params=pltpu.CompilerParams(
            collective_id=0, has_side_effects=True, vmem_limit_bytes=VMEM_LIMIT
        ),
    )(ancestor, selector, initial_state, perturbations, diffusivity, region_weight)
    return pl.pallas_call(
        finish,
        out_shape=(
            jax.ShapeDtypeStruct(initial_state.shape, f32),
            jax.ShapeDtypeStruct((1, 2), f32),
        ),
        in_specs=[scalar, near, near],
        out_specs=(far,) * 2,
        scratch_shapes=[dma((fields + 1,))],
        compiler_params=pltpu.CompilerParams(vmem_limit_bytes=1 << 20),
    )(ancestor, results, action)


def solution(mesh):
    in_specs = (
        P(("ens", "mem"), None, None, "lon", None),
        P(("ens", "mem")),
        P(("ens", "mem")),
        P("ens", None, None, "lon", None),
        P(None, "lon", None),
        P("lon", None),
    )
    out_specs = (P(("ens", "mem"), None, None, "lon", None), P(("ens", "mem"), None))
    return jax.shard_map(body, mesh=mesh, in_specs=in_specs, out_specs=out_specs, check_vma=False)
```

```python
import functools

import jax
import jax.numpy as jnp
from jax import lax
from jax.experimental import pallas as pl
from jax.experimental.pallas import tpu as pltpu
from jax.sharding import PartitionSpec as P

STEPS = 3
TIME_STEP = 0.2
EDGE = 8
VMEM_LIMIT = 60000000
MESH_ID = pl.DeviceIdType.MESH


def kernel(
    n, ring, anc_ref, sel_ref, init_ref, pert_ref, kap_ref, weight_ref, res_ref, act_ref,
    state, frame, mid, mid_e, kap, kap_frame, face, face_e, pert, noise, noise_e,
    pert_edge, pert_halo, stage, weight, ids, acc, block, spread, total, gather,
    i_send, i_recv, p_send, p_recv, z_send, z_recv, x_send, x_recv, g_send, g_recv,
    s_send, s_recv, local_sem, token,
):
    _, fields, levels, width, lat = init_ref.shape
    half = levels // 2
    pairs = n // 2
    top = width - EDGE
    outer = 3 * EDGE
    mem = lax.axis_index("mem")
    lon = lax.axis_index("lon")
    core = lax.rem(mem, 2)
    base = mem - core
    pair = mem // 2
    east, west = lax.rem(lon + 1, ring), lax.rem(lon + ring - 1, ring)
    mine = core * half
    relations = [(q, t) for q in range(pairs) for t in range(2)]

    def core_of(t):
        return core if t == 0 else 1 - core

    def target(q, t):
        return lax.rem(base + 2 * q, n) + core_of(t)

    local = [
        pltpu.make_async_copy(
            init_ref.at[0, :, pl.ds(mine, half)], state.at[core], local_sem.at[0]
        ),
        pltpu.make_async_copy(kap_ref.at[pl.ds(mine, half)], kap, local_sem.at[1]),
        pltpu.make_async_copy(weight_ref, weight, local_sem.at[2]),
        pltpu.make_async_copy(pert_ref.at[:, :, pl.ds(mine, half)], pert, local_sem.at[3]),
    ]

    barrier = pltpu.get_barrier_semaphore()
    for q, t in relations[1:]:
        pl.semaphore_signal(
            barrier, inc=1, device_id={"mem": target(q, t)}, device_id_type=MESH_ID
        )

    def toward(semaphore, up, t):
        @pl.when(lon < ring - 1 if up else lon > 0)
        def _():
            pl.semaphore_signal(
                semaphore,
                inc=1,
                device_id={"lon": east if up else west, "mem": target(0, t)},
                device_id_type=MESH_ID,
            )

    for t in range(2):
        toward(barrier, True, t)
        toward(barrier, False, t)
    for copy in local:
        copy.start()
    line = lax.broadcasted_iota(jnp.int32, (EDGE, lat), 0)
    ids[mem] = jnp.where(line == 0, anc_ref[0], sel_ref[0])
    beside = jnp.where(lon > 0, 1, 0) + jnp.where(lon < ring - 1, 1, 0)
    pl.semaphore_wait(barrier, n - 1 + 2 * beside)

    def pass_token(up):
        pl.semaphore_wait(token.at[int(up)], 1)
        toward(token.at[int(up)], up, 0)

    def send_ids(q, t):
        slot = 2 * q + t - 1
        return pltpu.make_async_remote_copy(
            src_ref=ids.at[mem],
            dst_ref=ids.at[mem],
            send_sem=i_send.at[slot],
            recv_sem=i_recv.at[slot],
            device_id={"mem": target(q, t)},
            device_id_type=MESH_ID,
        )

    to_twin = pltpu.make_async_remote_copy(
        src_ref=init_ref.at[0, :, pl.ds(half - mine, half)],
        dst_ref=state.at[core],
        send_sem=p_send,
        recv_sem=p_recv,
        device_id={"mem": target(0, 1)},
        device_id_type=MESH_ID,
    )

    def lon_copy(source, place, slot, side, t=0):
        return pltpu.make_async_remote_copy(
            src_ref=source,
            dst_ref=place,
            send_sem=z_send.at[slot, side],
            recv_sem=z_recv.at[slot, side],
            device_id={"lon": jnp.where(side == 1, east, west), "mem": target(0, t)},
            device_id_type=MESH_ID,
        )

    def edge_rows(w):
        return pl.ds(pl.multiple_of(top * w, EDGE), EDGE)

    def beyond(w):
        return pl.ds(pl.multiple_of(2 * EDGE * w, EDGE), EDGE)

    def halo(t, side):
        return lon_copy(
            init_ref.at[0, :, pl.ds(core_of(t) * half, half), edge_rows(side)],
            frame.at[1 - side, core, :, :, beyond(1 - side)],
            t,
            side,
            t,
        )

    def kap_copy(side):
        return lon_copy(
            kap_ref.at[pl.ds(mine, half), edge_rows(side)],
            kap_frame.at[1 - side, :, beyond(1 - side)],
            2,
            side,
        )

    def pert_copy(side):
        return lon_copy(pert_edge.at[side], pert_halo.at[1 - side], 3, side)

    def start_halo(side):
        halo(0, side).start()
        halo(1, side).start()
        kap_copy(side).start()

    for q, t in relations[1:]:
        send_ids(q, t).start()
    to_twin.start()
    for side, inside in enumerate((lon > 0, lon < ring - 1)):

        @pl.when(inside)
        def _():
            start_halo(side)

    lower = jnp.logical_and(lon > 0, 2 * lon < ring)
    upper = 2 * lon >= ring

    @pl.when(lon == 1)
    def _():
        toward(token.at[1], True, 0)

    @pl.when(lon == ring - 2)
    def _():
        toward(token.at[0], False, 0)

    @pl.when(jnp.logical_and(lower, lon > 1))
    def _():
        pass_token(True)

    lane = lax.broadcasted_iota(jnp.int32, (width, lat), 1)
    not_north = jnp.where(lane == lat - 1, 0.0, 1.0)
    not_south = jnp.where(lane == 0, 0.0, 1.0)

    def from_west(q):
        return pltpu.roll(q, 1, 0)

    def from_east(q):
        return pltpu.roll(q, q.shape[0] - 1, 0)

    def from_south(q):
        return pltpu.roll(q, 1, 1)

    def from_north(q):
        return pltpu.roll(q, lat - 1, 1)

    def put_faces(held, level, k):
        to_east = (0.5 * TIME_STEP) * (k + from_east(k))
        to_north = (0.5 * TIME_STEP) * (k + from_north(k)) * not_north[: k.shape[0]]
        held[0, level] = to_east
        held[1, level] = from_west(to_east)
        held[2, level] = to_north
        held[3, level] = from_south(to_north)

    def coefficients(u, v, held, level):
        size = u.shape[0]
        u = TIME_STEP * u
        v = TIME_STEP * v
        to_e = held[0, level] - jnp.minimum(u, 0.0)
        to_w = held[1, level] + jnp.maximum(u, 0.0)
        to_n = held[2, level] - jnp.minimum(v, 0.0) * not_north[:size]
        to_s = held[3, level] + jnp.maximum(v, 0.0) * not_south[:size]
        here = 1.0 - ((to_e + to_w) + (to_n + to_s))
        return to_e, to_w, to_n, to_s, here

    def moved(q, c):
        to_e, to_w, to_n, to_s, here = c
        return (
            here * q
            + (to_e * from_east(q) + to_w * from_west(q))
            + (to_n * from_north(q) + to_s * from_south(q))
        )

    def observed(t, share):
        terms = share * t * t
        return jnp.sum(terms.reshape(-1, 8, lat), axis=0)

    def look_inner(t):
        return observed(t[EDGE:top], weight[EDGE:top])

    def advance(states, held, spots, totals, look):
        for _ in range(STEPS):
            for k in range(len(states)):
                c = coefficients(states[k][0], states[k][1], held, spots[k])
                states[k] = [moved(q, c) for q in states[k]]
                totals[k] = totals[k] + look(states[k][2])
        return states, totals

    zero = jnp.zeros((8, lat), jnp.float32)

    def inner_member(t):
        a = core_of(t)
        states = [[state[a, f, level] for f in range(fields)] for level in range(half)]
        states, totals = advance(states, face, list(range(half)), [zero] * half, look_inner)
        for level in range(half):
            for f in range(fields):
                mid[a, f, level] = states[level][f]
        acc[t, 0] = functools.reduce(jnp.add, totals)

    for copy in local[:3]:
        copy.wait()
    for level in range(half):
        put_faces(face, level, kap[level])
    inner_member(0)

    kinds = pert.shape[0]
    packed = pert_edge.shape[2]
    used = half * fields * STEPS
    local[3].wait()

    def pack(j, carry):
        for level in range(half):
            for f in range(fields):
                spot = pl.ds((level * fields + f) * STEPS, STEPS)
                pert_edge[0, j, spot, :] = pert[j, f, level, 0:STEPS, :]
                pert_edge[1, j, spot, :] = pert[j, f, level, width - STEPS : width, :]
        if packed > used:
            for side in range(2):
                pert_edge[side, j, pl.ds(used, packed - used), :] = jnp.zeros(
                    (packed - used, lat), jnp.float32
                )
        return carry

    lax.fori_loop(0, kinds, pack, 0)
    for side, inside in enumerate((lon > 0, lon < ring - 1)):

        @pl.when(inside)
        def _():
            pert_copy(side).start()

    @pl.when(upper)
    def _():
        pass_token(True)

        @pl.when(lon < ring - 2)
        def _():
            pass_token(False)

        @pl.when(lon == ring - 1)
        def _():
            start_halo(1)
            pert_copy(1).start()

    @pl.when(lower)
    def _():
        pass_token(False)

    to_twin.wait_recv()
    inner_member(1)

    for q, t in relations[1:]:
        send_ids(q, t).wait_recv()

    def choose(q, t, level):
        chosen = ids[target(q, t), 1:2, :]
        for f in range(fields):
            value = pert[0, f, level]
            for j in range(1, kinds):
                value = jnp.where(chosen == j, pert[j, f, level], value)
            noise[2 * q + t, f, level] = value

    def piece(q, t, slot, levels_here, levels_there, rows):
        r = 2 * q + t
        return pltpu.make_async_remote_copy(
            src_ref=stage.at[r, :, levels_here, rows],
            dst_ref=res_ref.at[pair, :, levels_there, rows],
            send_sem=x_send.at[r - 1, slot],
            recv_sem=x_recv.at[r - 1, slot],
            device_id={"mem": target(q, t)},
            device_id_type=MESH_ID,
        )

    def inner_piece(q, t, level):
        return piece(q, t, level, level, mine + level, pl.ds(EDGE, top - EDGE))

    def outer_piece(q, t, w):
        return piece(q, t, half + w, pl.ds(0, half), pl.ds(mine, half), edge_rows(w))

    def put(q, t, f, level, rows, value):
        if (q, t) == (0, 0):
            res_ref[pair, f, mine + level, rows, :] = value
        else:
            stage[2 * q + t, f, level, rows, :] = value

    def second(q, t):
        return ids[target(q, t), 0:1, :] == base + 1

    def inner_clones(q):
        def one(level, totals):
            totals = list(totals)
            for t in range(2):
                choose(q, t, level)
                states = [
                    [
                        jnp.where(second(q, t), mid[1, f, level], mid[0, f, level])
                        + noise[2 * q + t, f, level]
                        for f in range(fields)
                    ]
                ]
                states, (totals[t],) = advance(states, face, [level], [totals[t]], look_inner)
                for f in range(fields):
                    put(q, t, f, level, slice(EDGE, top), states[0][f][EDGE:top])
                if (q, t) != (0, 0):
                    inner_piece(q, t, level).start()
            if q == 1:

                @pl.when(jnp.logical_and(lon == 0, level == 0))
                def _():
                    pl.semaphore_wait(token.at[0], 1)
                    start_halo(0)
                    pert_copy(0).start()

            return tuple(totals)

        totals = lax.fori_loop(0, half, one, (zero, zero))
        for t in range(2):
            acc[2 * q + t, 1] = totals[t]

    for q in range(1, pairs):
        inner_clones(q)

    inner_clones(0)

    blank = jnp.zeros((EDGE - STEPS, lat), jnp.float32)

    def outer_rows(turn, carry):
        w = jnp.where(lon == 0, 1 - turn, turn)
        here = pl.ds(pl.multiple_of(EDGE * (1 - w), EDGE), 2 * EDGE)
        there = pl.ds(pl.multiple_of((width - 2 * EDGE) * w, EDGE), 2 * EDGE)

        def look_outer(t):
            return observed(t[EDGE : 2 * EDGE], weight[edge_rows(w)])

        kap_copy(1 - w).wait_recv()
        halo(0, 1 - w).wait_recv()
        halo(1, 1 - w).wait_recv()

        spots = [(level, t) for level in range(half) for t in range(2)]
        states = []
        for level in range(half):
            kap_frame[w, level, here, :] = kap[level, there, :]
            put_faces(face_e, level, kap_frame[w, level])
        for level, t in spots:
            for f in range(fields):
                frame[w, core_of(t), f, level, here, :] = state[core_of(t), f, level, there, :]
            states.append([frame[w, core_of(t), f, level] for f in range(fields)])
        grounds = [level for level, _ in spots]
        states, totals = advance(states, face_e, grounds, [zero] * len(spots), look_outer)
        for (level, t), fresh, total_of in zip(spots, states, totals):
            for f in range(fields):
                mid_e[core_of(t), f, level] = fresh[f]
            acc[t, 0] = acc[t, 0] + total_of
        pert_copy(1 - w).wait_recv()

        for q in list(range(1, pairs)) + [0]:

            states = []
            for level, t in spots:
                r = 2 * q + t
                chosen = ids[target(q, t), 1:2, :]
                ends = pert_halo[w, 0]
                for j in range(1, kinds):
                    ends = jnp.where(chosen == j, pert_halo[w, j], ends)
                fresh = []
                for f in range(fields):
                    start = (level * fields + f) * STEPS
                    rim = ends[start : start + STEPS]
                    noise_e[level, t, f, here, :] = noise[r, f, level, there, :]
                    noise_e[level, t, f, beyond(w), :] = jnp.where(
                        w == 0,
                        jnp.concatenate([blank, rim], axis=0),
                        jnp.concatenate([rim, blank], axis=0),
                    )
                    fresh.append(
                        jnp.where(second(q, t), mid_e[1, f, level], mid_e[0, f, level])
                        + noise_e[level, t, f]
                    )
                states.append(fresh)
            states, totals = advance(states, face_e, grounds, [zero] * len(spots), look_outer)
            for (level, t), fresh, total_of in zip(spots, states, totals):
                for f in range(fields):
                    put(q, t, f, level, edge_rows(w), fresh[f][EDGE : 2 * EDGE])
                acc[2 * q + t, 1] = acc[2 * q + t, 1] + total_of
            for t in range(2):
                if (q, t) != (0, 0):
                    outer_piece(q, t, w).start()
        return carry

    lax.fori_loop(0, 2, outer_rows, 0)
    for q, t in relations:
        r = 2 * q + t
        ancestor = ids[target(q, t), 0:1, :]
        held = jnp.logical_or(ancestor == base, ancestor == base + 1)
        acc[r, 1] = jnp.where(held, acc[r, 1], 0.0)
        if q:
            acc[r, 0] = zero

    block[...] = jnp.concatenate(
        [
            jnp.sum(acc[2 * q + t, which], axis=0, keepdims=True)
            for q, t in relations
            for which in range(2)
        ],
        axis=0,
    )
    spread[lon] = block[...]
    shares = [
        pltpu.make_async_remote_copy(
            src_ref=block,
            dst_ref=spread.at[lon],
            send_sem=s_send.at[d - 1],
            recv_sem=s_recv.at[d - 1],
            device_id={"lon": lax.rem(lon + d, ring)},
            device_id_type=MESH_ID,
        )
        for d in range(1, ring)
    ]
    for copy in shares:
        copy.start()
    for copy in shares:
        copy.wait_recv()

    def hand(q, t):
        r = 2 * q + t
        return pltpu.make_async_remote_copy(
            src_ref=total,
            dst_ref=gather.at[r],
            send_sem=g_send.at[r - 1],
            recv_sem=g_recv.at[r - 1],
            device_id={"mem": target(q, t)},
            device_id_type=MESH_ID,
        )

    whole = jnp.sum(spread[...], axis=0)
    total[...] = whole
    gather[0] = whole
    for q, t in relations[1:]:
        hand(q, t).start()
    for q, t in relations[1:]:
        hand(q, t).wait_recv()
    cells = levels * lat * width * ring
    pair_of = functools.reduce(jnp.add, [gather[r, 2 * r : 2 * r + 2, :] for r in range(n)])
    summed = jnp.sum(pair_of, axis=1, keepdims=True) / cells
    column = lax.broadcasted_iota(jnp.int32, (1, 2), 1)
    act_ref[...] = jnp.where(column == 0, summed[0:1], summed[1:2])

    for copy in shares:
        copy.wait_send()
    for q, t in relations[1:]:
        hand(q, t).wait_send()
    for q, t in relations[1:]:
        send_ids(q, t).wait_send()
    to_twin.wait_send()
    for side in range(2):
        kap_copy(side).wait_send()
        pert_copy(side).wait_send()
        for t in range(2):
            halo(t, side).wait_send()
    for q, t in relations[1:]:
        for level in range(half):
            inner_piece(q, t, level).wait()
        for w in range(2):
            outer_piece(q, t, w).wait()


def finish(anc_ref, res_ref, action_ref, state_out, action_out, sem):
    fields = res_ref.shape[1]
    chosen = anc_ref[0] // 2
    copies = [
        pltpu.make_async_copy(res_ref.at[chosen, f], state_out.at[0, f], sem.at[f])
        for f in range(fields)
    ]
    copies.append(pltpu.make_async_copy(action_ref, action_out, sem.at[fields]))
    for copy in copies:
        copy.start()
    for copy in copies:
        copy.wait()


def body(initial_state, ancestor, selector, perturbations, diffusivity, region_weight):
    n, ring = lax.axis_size("mem"), lax.axis_size("lon")
    _, fields, levels, width, lat = initial_state.shape
    half, pairs = levels // 2, n // 2
    kinds = perturbations.shape[0]
    outer = 3 * EDGE
    packed = -(-half * fields * STEPS // 8) * 8
    f32 = jnp.float32
    far = pl.BlockSpec(memory_space=pltpu.HBM)
    near = pl.BlockSpec(memory_space=pltpu.VMEM)
    scalar = pl.BlockSpec(memory_space=pltpu.SMEM)
    dma = pltpu.SemaphoreType.DMA
    results, action = pl.pallas_call(
        functools.partial(kernel, n, ring),
        out_shape=(
            pltpu.VMEM((pairs, fields, levels, width, lat), f32),
            pltpu.VMEM((1, 2), f32),
        ),
        in_specs=[scalar] * 2 + [far] * 4,
        out_specs=(near,) * 2,
        scratch_shapes=[
            pltpu.VMEM((2, fields, half, width, lat), f32),
            pltpu.VMEM((2, 2, fields, half, outer, lat), f32),
            pltpu.VMEM((2, fields, half, width, lat), f32),
            pltpu.VMEM((2, fields, half, outer, lat), f32),
            pltpu.VMEM((half, width, lat), f32),
            pltpu.VMEM((2, half, outer, lat), f32),
            pltpu.VMEM((4, half, width, lat), f32),
            pltpu.VMEM((4, half, outer, lat), f32),
            pltpu.VMEM((kinds, fields, half, width, lat), f32),
            pltpu.VMEM((n, fields, half, width, lat), f32),
            pltpu.VMEM((half, 2, fields, outer, lat), f32),
            pltpu.VMEM((2, kinds, packed, lat), f32),
            pltpu.VMEM((2, kinds, packed, lat), f32),
            pltpu.VMEM((n, fields, half, width, lat), f32),
            pltpu.VMEM((width, lat), f32),
            pltpu.VMEM((n, EDGE, lat), jnp.int32),
            pltpu.VMEM((n, 2, 8, lat), f32),
            pltpu.VMEM((2 * n, lat), f32),
            pltpu.VMEM((ring, 2 * n, lat), f32),
            pltpu.VMEM((2 * n, lat), f32),
            pltpu.VMEM((n, 2 * n, lat), f32),
            dma((n - 1,)),
            dma((n - 1,)),
            dma,
            dma,
            dma((4, 2)),
            dma((4, 2)),
            dma((n - 1, half + 2)),
            dma((n - 1, half + 2)),
            dma((n - 1,)),
            dma((n - 1,)),
            dma((ring - 1,)),
            dma((ring - 1,)),
            dma((4,)),
            pltpu.SemaphoreType.REGULAR((2,)),
        ],
        compiler_params=pltpu.CompilerParams(
            collective_id=0, has_side_effects=True, vmem_limit_bytes=VMEM_LIMIT
        ),
    )(ancestor, selector, initial_state, perturbations, diffusivity, region_weight)
    return pl.pallas_call(
        finish,
        out_shape=(
            jax.ShapeDtypeStruct(initial_state.shape, f32),
            jax.ShapeDtypeStruct((1, 2), f32),
        ),
        in_specs=[scalar, near, near],
        out_specs=(far,) * 2,
        scratch_shapes=[dma((fields + 1,))],
        compiler_params=pltpu.CompilerParams(vmem_limit_bytes=1 << 20),
    )(ancestor, results, action)


def solution(mesh):
    in_specs = (
        P(("ens", "mem"), None, None, "lon", None),
        P(("ens", "mem")),
        P(("ens", "mem")),
        P("ens", None, None, "lon", None),
        P(None, "lon", None),
        P("lon", None),
    )
    out_specs = (P(("ens", "mem"), None, None, "lon", None), P(("ens", "mem"), None))
    return jax.shard_map(body, mesh=mesh, in_specs=in_specs, out_specs=out_specs, check_vma=False)
```

```python
import functools

import jax
import jax.numpy as jnp
from jax import lax
from jax.experimental import pallas as pl
from jax.experimental.pallas import tpu as pltpu
from jax.sharding import PartitionSpec as P

STEPS = 3
TIME_STEP = 0.2
EDGE = 8
VMEM_LIMIT = 60000000
MESH_ID = pl.DeviceIdType.MESH


def kernel(
    n, ring, anc_ref, sel_ref, init_ref, pert_ref, kap_ref, weight_ref, res_ref, act_ref,
    state, frame, mid, mid_e, kap, kap_frame, face, face_e, pert, noise, noise_e,
    mid_h, coef_m, coef_c,
    pert_edge, pert_halo, stage, weight, ids, acc, block, spread, total, gather,
    i_send, i_recv, p_send, p_recv, z_send, z_recv, x_send, x_recv, g_send, g_recv,
    s_send, s_recv, local_sem, token,
):
    _, fields, levels, width, lat = init_ref.shape
    half = levels // 2
    pairs = n // 2
    top = width - EDGE
    outer = 3 * EDGE
    mem = lax.axis_index("mem")
    lon = lax.axis_index("lon")
    core = lax.rem(mem, 2)
    base = mem - core
    pair = mem // 2
    east, west = lax.rem(lon + 1, ring), lax.rem(lon + ring - 1, ring)
    mine = core * half
    relations = [(q, t) for q in range(pairs) for t in range(2)]

    def core_of(t):
        return core if t == 0 else 1 - core

    def target(q, t):
        return lax.rem(base + 2 * q, n) + core_of(t)

    local = [
        pltpu.make_async_copy(
            init_ref.at[0, :, pl.ds(mine, half)], state.at[core], local_sem.at[0]
        ),
        pltpu.make_async_copy(kap_ref.at[pl.ds(mine, half)], kap, local_sem.at[1]),
        pltpu.make_async_copy(weight_ref, weight, local_sem.at[2]),
        pltpu.make_async_copy(pert_ref.at[:, :, pl.ds(mine, half)], pert, local_sem.at[3]),
    ]

    barrier = pltpu.get_barrier_semaphore()
    for q, t in relations[1:]:
        pl.semaphore_signal(
            barrier, inc=1, device_id={"mem": target(q, t)}, device_id_type=MESH_ID
        )

    def toward(semaphore, up, t):
        @pl.when(lon < ring - 1 if up else lon > 0)
        def _():
            pl.semaphore_signal(
                semaphore,
                inc=1,
                device_id={"lon": east if up else west, "mem": target(0, t)},
                device_id_type=MESH_ID,
            )

    for t in range(2):
        toward(barrier, True, t)
        toward(barrier, False, t)
    for copy in local:
        copy.start()
    line = lax.broadcasted_iota(jnp.int32, (EDGE, lat), 0)
    ids[mem] = jnp.where(line == 0, anc_ref[0], sel_ref[0])
    beside = jnp.where(lon > 0, 1, 0) + jnp.where(lon < ring - 1, 1, 0)
    pl.semaphore_wait(barrier, n - 1 + 2 * beside)

    def pass_token(up):
        pl.semaphore_wait(token.at[int(up)], 1)
        toward(token.at[int(up)], up, 0)

    def send_ids(q, t):
        slot = 2 * q + t - 1
        return pltpu.make_async_remote_copy(
            src_ref=ids.at[mem],
            dst_ref=ids.at[mem],
            send_sem=i_send.at[slot],
            recv_sem=i_recv.at[slot],
            device_id={"mem": target(q, t)},
            device_id_type=MESH_ID,
        )

    to_twin = pltpu.make_async_remote_copy(
        src_ref=init_ref.at[0, :, pl.ds(half - mine, half)],
        dst_ref=state.at[core],
        send_sem=p_send,
        recv_sem=p_recv,
        device_id={"mem": target(0, 1)},
        device_id_type=MESH_ID,
    )

    def lon_copy(source, place, slot, side, t=0):
        return pltpu.make_async_remote_copy(
            src_ref=source,
            dst_ref=place,
            send_sem=z_send.at[slot, side],
            recv_sem=z_recv.at[slot, side],
            device_id={"lon": jnp.where(side == 1, east, west), "mem": target(0, t)},
            device_id_type=MESH_ID,
        )

    def edge_rows(w):
        return pl.ds(pl.multiple_of(top * w, EDGE), EDGE)

    def beyond(w):
        return pl.ds(pl.multiple_of(2 * EDGE * w, EDGE), EDGE)

    dyn = fields - 1

    def halo(t, side, humid=False):
        which = pl.ds(dyn, 1) if humid else pl.ds(0, dyn)
        return lon_copy(
            init_ref.at[0, which, pl.ds(core_of(t) * half, half), edge_rows(side)],
            frame.at[1 - side, core, which, :, beyond(1 - side)],
            4 + t if humid else t,
            side,
            t,
        )

    def kap_copy(side):
        return lon_copy(
            kap_ref.at[pl.ds(mine, half), edge_rows(side)],
            kap_frame.at[1 - side, :, beyond(1 - side)],
            2,
            side,
        )

    def pert_copy(side):
        return lon_copy(pert_edge.at[side], pert_halo.at[1 - side], 3, side)

    def start_halo(side):
        halo(0, side).start()
        halo(1, side).start()
        kap_copy(side).start()

    def start_rims(side):
        pert_copy(side).start()
        halo(0, side, True).start()
        halo(1, side, True).start()

    for q, t in relations[1:]:
        send_ids(q, t).start()
    to_twin.start()
    for side, inside in enumerate((lon > 0, lon < ring - 1)):

        @pl.when(inside)
        def _():
            start_halo(side)

    lower = jnp.logical_and(lon > 0, 2 * lon < ring)
    upper = 2 * lon >= ring

    @pl.when(lon == 1)
    def _():
        toward(token.at[1], True, 0)

    @pl.when(lon == ring - 2)
    def _():
        toward(token.at[0], False, 0)

    @pl.when(jnp.logical_and(lower, lon > 1))
    def _():
        pass_token(True)

    lane = lax.broadcasted_iota(jnp.int32, (width, lat), 1)
    not_north = jnp.where(lane == lat - 1, 0.0, 1.0)
    not_south = jnp.where(lane == 0, 0.0, 1.0)

    def from_west(q):
        return pltpu.roll(q, 1, 0)

    def from_east(q):
        return pltpu.roll(q, q.shape[0] - 1, 0)

    def from_south(q):
        return pltpu.roll(q, 1, 1)

    def from_north(q):
        return pltpu.roll(q, lat - 1, 1)

    def put_faces(held, level, k):
        to_east = (0.5 * TIME_STEP) * (k + from_east(k))
        to_north = (0.5 * TIME_STEP) * (k + from_north(k)) * not_north[: k.shape[0]]
        held[0, level] = to_east
        held[1, level] = from_west(to_east)
        held[2, level] = to_north
        held[3, level] = from_south(to_north)

    def coefficients(u, v, held, level):
        size = u.shape[0]
        u = TIME_STEP * u
        v = TIME_STEP * v
        to_e = held[0, level] - jnp.minimum(u, 0.0)
        to_w = held[1, level] + jnp.maximum(u, 0.0)
        to_n = held[2, level] - jnp.minimum(v, 0.0) * not_north[:size]
        to_s = held[3, level] + jnp.maximum(v, 0.0) * not_south[:size]
        here = 1.0 - ((to_e + to_w) + (to_n + to_s))
        return to_e, to_w, to_n, to_s, here

    def moved(q, c):
        to_e, to_w, to_n, to_s, here = c
        return (
            here * q
            + (to_e * from_east(q) + to_w * from_west(q))
            + (to_n * from_north(q) + to_s * from_south(q))
        )

    def observed(t, share):
        terms = share * t * t
        return jnp.sum(terms.reshape(-1, 8, lat), axis=0)

    def look_inner(t):
        return observed(t[EDGE:top], weight[EDGE:top])

    def advance(states, held, spots, totals, look, keep=None):
        for step in range(STEPS):
            for k in range(len(states)):
                c = coefficients(states[k][0], states[k][1], held, spots[k])
                if keep is not None:
                    for i in range(5):
                        keep[k, step, i] = c[i]
                states[k] = [moved(q, c) for q in states[k]]
                totals[k] = totals[k] + look(states[k][2])
        return states, totals

    zero = jnp.zeros((8, lat), jnp.float32)

    def inner_member(t):
        a = core_of(t)
        states = [[state[a, f, level] for f in range(fields)] for level in range(half)]
        states, totals = advance(states, face, list(range(half)), [zero] * half, look_inner)
        for level in range(half):
            for f in range(fields):
                mid[a, f, level] = states[level][f]
        acc[t, 0] = functools.reduce(jnp.add, totals)

    for copy in local[:3]:
        copy.wait()
    for level in range(half):
        put_faces(face, level, kap[level])
    inner_member(0)

    kinds = pert.shape[0]
    packed = pert_edge.shape[2]
    used = half * fields * STEPS
    local[3].wait()

    def pack(j, carry):
        for level in range(half):
            for f in range(fields):
                spot = pl.ds((level * fields + f) * STEPS, STEPS)
                pert_edge[0, j, spot, :] = pert[j, f, level, 0:STEPS, :]
                pert_edge[1, j, spot, :] = pert[j, f, level, width - STEPS : width, :]
        if packed > used:
            for side in range(2):
                pert_edge[side, j, pl.ds(used, packed - used), :] = jnp.zeros(
                    (packed - used, lat), jnp.float32
                )
        return carry

    lax.fori_loop(0, kinds, pack, 0)
    for side, inside in enumerate((lon > 0, lon < ring - 1)):

        @pl.when(inside)
        def _():
            start_rims(side)

    @pl.when(upper)
    def _():
        pass_token(True)

        @pl.when(lon < ring - 2)
        def _():
            pass_token(False)

        @pl.when(lon == ring - 1)
        def _():
            start_halo(1)
            start_rims(1)

    @pl.when(lower)
    def _():
        pass_token(False)

    to_twin.wait_recv()
    inner_member(1)

    for q, t in relations[1:]:
        send_ids(q, t).wait_recv()

    def choose(q, t, level):
        chosen = ids[target(q, t), 1:2, :]
        for f in range(fields):
            value = pert[0, f, level]
            for j in range(1, kinds):
                value = jnp.where(chosen == j, pert[j, f, level], value)
            noise[2 * q + t, f, level] = value

    def piece(q, t, slot, levels_here, levels_there, rows):
        r = 2 * q + t
        return pltpu.make_async_remote_copy(
            src_ref=stage.at[r, :, levels_here, rows],
            dst_ref=res_ref.at[pair, :, levels_there, rows],
            send_sem=x_send.at[r - 1, slot],
            recv_sem=x_recv.at[r - 1, slot],
            device_id={"mem": target(q, t)},
            device_id_type=MESH_ID,
        )

    def inner_piece(q, t, level):
        return piece(q, t, level, level, mine + level, pl.ds(EDGE, top - EDGE))

    def outer_piece(q, t, w):
        return piece(q, t, half + w, pl.ds(0, half), pl.ds(mine, half), edge_rows(w))

    def put(q, t, f, level, rows, value):
        if (q, t) == (0, 0):
            res_ref[pair, f, mine + level, rows, :] = value
        else:
            stage[2 * q + t, f, level, rows, :] = value

    def second(q, t):
        return ids[target(q, t), 0:1, :] == base + 1

    def inner_clones(q):
        def one(level, totals):
            totals = list(totals)
            for t in range(2):
                choose(q, t, level)
                states = [
                    [
                        jnp.where(second(q, t), mid[1, f, level], mid[0, f, level])
                        + noise[2 * q + t, f, level]
                        for f in range(fields)
                    ]
                ]
                states, (totals[t],) = advance(states, face, [level], [totals[t]], look_inner)
                for f in range(fields):
                    put(q, t, f, level, slice(EDGE, top), states[0][f][EDGE:top])
                if (q, t) != (0, 0):
                    inner_piece(q, t, level).start()
            if q == 1:

                @pl.when(jnp.logical_and(lon == 0, level == 0))
                def _():
                    pl.semaphore_wait(token.at[0], 1)
                    start_halo(0)
                    start_rims(0)

            return tuple(totals)

        totals = lax.fori_loop(0, half, one, (zero, zero))
        for t in range(2):
            acc[2 * q + t, 1] = totals[t]

    for q in range(1, pairs):
        inner_clones(q)

    inner_clones(0)

    blank = jnp.zeros((EDGE - STEPS, lat), jnp.float32)
    spots = [(level, t) for level in range(half) for t in range(2)]

    def outer_rows(turn, carry):
        w = jnp.where(lon == 0, 1 - turn, turn)
        here = pl.ds(pl.multiple_of(EDGE * (1 - w), EDGE), 2 * EDGE)
        there = pl.ds(pl.multiple_of((width - 2 * EDGE) * w, EDGE), 2 * EDGE)

        def look_outer(t):
            return observed(t[EDGE : 2 * EDGE], weight[edge_rows(w)])

        kap_copy(1 - w).wait_recv()
        halo(0, 1 - w).wait_recv()
        halo(1, 1 - w).wait_recv()

        states = []
        for level in range(half):
            kap_frame[w, level, here, :] = kap[level, there, :]
            put_faces(face_e, level, kap_frame[w, level])
        for level, t in spots:
            for f in range(dyn):
                frame[w, core_of(t), f, level, here, :] = state[core_of(t), f, level, there, :]
            states.append([frame[w, core_of(t), f, level] for f in range(dyn)])
        grounds = [level for level, _ in spots]
        nothing = [zero] * len(spots)
        states, totals = advance(states, face_e, grounds, list(nothing), look_outer, coef_m.at[w])
        for (level, t), fresh, total_of in zip(spots, states, totals):
            for f in range(dyn):
                mid_e[core_of(t), f, level] = fresh[f]
            acc[t, 0] = acc[t, 0] + total_of
        pert_copy(1 - w).wait_recv()

        for q in list(range(1, pairs)) + [0]:
            states = []
            for level, t in spots:
                r = 2 * q + t
                chosen = ids[target(q, t), 1:2, :]
                ends = pert_halo[w, 0]
                for j in range(1, kinds):
                    ends = jnp.where(chosen == j, pert_halo[w, j], ends)
                fresh = []
                for f in range(dyn):
                    start = (level * fields + f) * STEPS
                    rim = ends[start : start + STEPS]
                    noise_e[level, t, f, here, :] = noise[r, f, level, there, :]
                    noise_e[level, t, f, beyond(w), :] = jnp.where(
                        w == 0,
                        jnp.concatenate([blank, rim], axis=0),
                        jnp.concatenate([rim, blank], axis=0),
                    )
                    fresh.append(
                        jnp.where(second(q, t), mid_e[1, f, level], mid_e[0, f, level])
                        + noise_e[level, t, f]
                    )
                states.append(fresh)
            states, totals = advance(
                states, face_e, grounds, list(nothing), look_outer, coef_c.at[w, q]
            )
            for (level, t), fresh, total_of in zip(spots, states, totals):
                for f in range(dyn):
                    put(q, t, f, level, edge_rows(w), fresh[f][EDGE : 2 * EDGE])
                acc[2 * q + t, 1] = acc[2 * q + t, 1] + total_of
        return carry

    lax.fori_loop(0, 2, outer_rows, 0)
    for q, t in relations:
        r = 2 * q + t
        ancestor = ids[target(q, t), 0:1, :]
        held = jnp.logical_or(ancestor == base, ancestor == base + 1)
        acc[r, 1] = jnp.where(held, acc[r, 1], 0.0)
        if q:
            acc[r, 0] = zero

    block[...] = jnp.concatenate(
        [
            jnp.sum(acc[2 * q + t, which], axis=0, keepdims=True)
            for q, t in relations
            for which in range(2)
        ],
        axis=0,
    )
    spread[lon] = block[...]
    shares = [
        pltpu.make_async_remote_copy(
            src_ref=block,
            dst_ref=spread.at[lon],
            send_sem=s_send.at[d - 1],
            recv_sem=s_recv.at[d - 1],
            device_id={"lon": lax.rem(lon + d, ring)},
            device_id_type=MESH_ID,
        )
        for d in range(1, ring)
    ]
    for copy in shares:
        copy.start()

    def glide(values, kept):
        for step in range(STEPS):
            for k in range(len(values)):
                values[k] = moved(values[k], [kept[k][step, i] for i in range(5)])
        return values

    places = [(w, x) for w in range(2) for x in range(len(spots))]
    values = []
    for w, x in places:
        level, t = spots[x]
        if x == 0:
            for side_t in range(2):
                halo(side_t, 1 - w, True).wait_recv()
        shore = pl.ds((width - 2 * EDGE) * w, 2 * EDGE)
        own_rows = state[core_of(t), dyn, level, shore, :]
        rim = frame[w, core_of(t), dyn, level, 2 * EDGE * w : 2 * EDGE * w + EDGE, :]
        values.append(jnp.concatenate([own_rows, rim] if w else [rim, own_rows], axis=0))
    values = glide(values, [coef_m.at[w, x] for w, x in places])
    for (w, x), value in zip(places, values):
        level, t = spots[x]
        mid_h[w, core_of(t), level] = value
    for q in list(range(1, pairs)) + [0]:
        values = []
        for w, x in places:
            level, t = spots[x]
            chosen = ids[target(q, t), 1:2, :]
            start = (level * fields + dyn) * STEPS
            rim = pert_halo[w, 0, start : start + STEPS, :]
            for j in range(1, kinds):
                rim = jnp.where(chosen == j, pert_halo[w, j, start : start + STEPS, :], rim)
            shore = pl.ds((width - 2 * EDGE) * w, 2 * EDGE)
            own_rows = noise[2 * q + t, dyn, level, shore, :]
            parts = [own_rows, rim, blank] if w else [blank, rim, own_rows]
            values.append(
                jnp.where(second(q, t), mid_h[w, 1, level], mid_h[w, 0, level])
                + jnp.concatenate(parts, axis=0)
            )
        values = glide(values, [coef_c.at[w, q, x] for w, x in places])
        for (w, x), value in zip(places, values):
            level, t = spots[x]
            put(q, t, dyn, level, edge_rows(w), value[EDGE : 2 * EDGE])
        for t in range(2):
            if (q, t) != (0, 0):
                outer_piece(q, t, 0).start()
                if (q, t) != (pairs - 1, 1):
                    outer_piece(q, t, 1).start()

    for q, t in relations[1:]:
        send_ids(q, t).wait_send()
    for side in range(2):
        kap_copy(side).wait_send()
        pert_copy(side).wait_send()
        for t in range(2):
            halo(t, side).wait_send()
            halo(t, side, True).wait_send()
    to_twin.wait_send()
    for copy in shares:
        copy.wait_recv()

    def hand(q, t):
        r = 2 * q + t
        return pltpu.make_async_remote_copy(
            src_ref=total,
            dst_ref=gather.at[r],
            send_sem=g_send.at[r - 1],
            recv_sem=g_recv.at[r - 1],
            device_id={"mem": target(q, t)},
            device_id_type=MESH_ID,
        )

    whole = jnp.sum(spread[...], axis=0)
    total[...] = whole
    gather[0] = whole
    for q, t in relations[1:]:
        hand(q, t).start()
    outer_piece(pairs - 1, 1, 1).start()
    for copy in shares:
        copy.wait_send()
    for q, t in relations[1:]:
        for level in range(half):
            inner_piece(q, t, level).wait()
    for q, t in relations[1:]:
        for w in range(2):
            outer_piece(q, t, w).wait()
    for q, t in relations[1:]:
        hand(q, t).wait_send()
    for q, t in relations[1:]:
        hand(q, t).wait_recv()
    cells = levels * lat * width * ring
    pair_of = functools.reduce(jnp.add, [gather[r, 2 * r : 2 * r + 2, :] for r in range(n)])
    summed = jnp.sum(pair_of, axis=1, keepdims=True) / cells
    column = lax.broadcasted_iota(jnp.int32, (1, 2), 1)
    act_ref[...] = jnp.where(column == 0, summed[0:1], summed[1:2])


def finish(anc_ref, res_ref, action_ref, state_out, action_out, sem):
    fields = res_ref.shape[1]
    chosen = anc_ref[0] // 2
    copies = [
        pltpu.make_async_copy(res_ref.at[chosen, f], state_out.at[0, f], sem.at[f])
        for f in range(fields)
    ]
    copies.append(pltpu.make_async_copy(action_ref, action_out, sem.at[fields]))
    for copy in copies:
        copy.start()
    for copy in copies:
        copy.wait()


def body(initial_state, ancestor, selector, perturbations, diffusivity, region_weight):
    n, ring = lax.axis_size("mem"), lax.axis_size("lon")
    _, fields, levels, width, lat = initial_state.shape
    half, pairs = levels // 2, n // 2
    kinds = perturbations.shape[0]
    outer = 3 * EDGE
    packed = -(-half * fields * STEPS // 8) * 8
    f32 = jnp.float32
    far = pl.BlockSpec(memory_space=pltpu.HBM)
    near = pl.BlockSpec(memory_space=pltpu.VMEM)
    scalar = pl.BlockSpec(memory_space=pltpu.SMEM)
    dma = pltpu.SemaphoreType.DMA
    results, action = pl.pallas_call(
        functools.partial(kernel, n, ring),
        out_shape=(
            pltpu.VMEM((pairs, fields, levels, width, lat), f32),
            pltpu.VMEM((1, 2), f32),
        ),
        in_specs=[scalar] * 2 + [far] * 4,
        out_specs=(near,) * 2,
        scratch_shapes=[
            pltpu.VMEM((2, fields, half, width, lat), f32),
            pltpu.VMEM((2, 2, fields, half, outer, lat), f32),
            pltpu.VMEM((2, fields, half, width, lat), f32),
            pltpu.VMEM((2, fields, half, outer, lat), f32),
            pltpu.VMEM((half, width, lat), f32),
            pltpu.VMEM((2, half, outer, lat), f32),
            pltpu.VMEM((4, half, width, lat), f32),
            pltpu.VMEM((4, half, outer, lat), f32),
            pltpu.VMEM((kinds, fields, half, width, lat), f32),
            pltpu.VMEM((n, fields, half, width, lat), f32),
            pltpu.VMEM((half, 2, fields - 1, outer, lat), f32),
            pltpu.VMEM((2, 2, half, outer, lat), f32),
            pltpu.VMEM((2, 2 * half, STEPS, 5, outer, lat), f32),
            pltpu.VMEM((2, pairs, 2 * half, STEPS, 5, outer, lat), f32),
            pltpu.VMEM((2, kinds, packed, lat), f32),
            pltpu.VMEM((2, kinds, packed, lat), f32),
            pltpu.VMEM((n, fields, half, width, lat), f32),
            pltpu.VMEM((width, lat), f32),
            pltpu.VMEM((n, EDGE, lat), jnp.int32),
            pltpu.VMEM((n, 2, 8, lat), f32),
            pltpu.VMEM((2 * n, lat), f32),
            pltpu.VMEM((ring, 2 * n, lat), f32),
            pltpu.VMEM((2 * n, lat), f32),
            pltpu.VMEM((n, 2 * n, lat), f32),
            dma((n - 1,)),
            dma((n - 1,)),
            dma,
            dma,
            dma((6, 2)),
            dma((6, 2)),
            dma((n - 1, half + 2)),
            dma((n - 1, half + 2)),
            dma((n - 1,)),
            dma((n - 1,)),
            dma((ring - 1,)),
            dma((ring - 1,)),
            dma((4,)),
            pltpu.SemaphoreType.REGULAR((2,)),
        ],
        compiler_params=pltpu.CompilerParams(
            collective_id=0, has_side_effects=True, vmem_limit_bytes=VMEM_LIMIT
        ),
    )(ancestor, selector, initial_state, perturbations, diffusivity, region_weight)
    return pl.pallas_call(
        finish,
        out_shape=(
            jax.ShapeDtypeStruct(initial_state.shape, f32),
            jax.ShapeDtypeStruct((1, 2), f32),
        ),
        in_specs=[scalar, near, near],
        out_specs=(far,) * 2,
        scratch_shapes=[dma((fields + 1,))],
        compiler_params=pltpu.CompilerParams(vmem_limit_bytes=1 << 20),
    )(ancestor, results, action)


def solution(mesh):
    in_specs = (
        P(("ens", "mem"), None, None, "lon", None),
        P(("ens", "mem")),
        P(("ens", "mem")),
        P("ens", None, None, "lon", None),
        P(None, "lon", None),
        P("lon", None),
    )
    out_specs = (P(("ens", "mem"), None, None, "lon", None), P(("ens", "mem"), None))
    return jax.shard_map(body, mesh=mesh, in_specs=in_specs, out_specs=out_specs, check_vma=False)
```

```python
import functools

import jax
import jax.numpy as jnp
from jax import lax
from jax.experimental import pallas as pl
from jax.experimental.pallas import tpu as pltpu
from jax.sharding import PartitionSpec as P

STEPS = 3
TIME_STEP = 0.2
EDGE = 8
VMEM_LIMIT = 60000000
MESH_ID = pl.DeviceIdType.MESH


def kernel(
    n, ring, anc_ref, sel_ref, init_ref, pert_ref, kap_ref, weight_ref, res_ref, act_ref,
    state, frame, mid, mid_e, kap, kap_frame, face, face_e, pert, noise, noise_e,
    mid_h, coef_m, coef_c,
    pert_edge, pert_halo, stage, weight, ids, acc, block, spread, total, gather,
    i_send, i_recv, p_send, p_recv, z_send, z_recv, x_send, x_recv, g_send, g_recv,
    s_send, s_recv, local_sem, token,
):
    _, fields, levels, width, lat = init_ref.shape
    half = levels // 2
    pairs = n // 2
    top = width - EDGE
    outer = 3 * EDGE
    mem = lax.axis_index("mem")
    lon = lax.axis_index("lon")
    core = lax.rem(mem, 2)
    base = mem - core
    pair = mem // 2
    east, west = lax.rem(lon + 1, ring), lax.rem(lon + ring - 1, ring)
    mine = core * half
    relations = [(q, t) for q in range(pairs) for t in range(2)]

    def core_of(t):
        return core if t == 0 else 1 - core

    def target(q, t):
        return lax.rem(base + 2 * q, n) + core_of(t)

    local = [
        pltpu.make_async_copy(
            init_ref.at[0, :, pl.ds(mine, half)], state.at[core], local_sem.at[0]
        ),
        pltpu.make_async_copy(kap_ref.at[pl.ds(mine, half)], kap, local_sem.at[1]),
        pltpu.make_async_copy(weight_ref, weight, local_sem.at[2]),
        pltpu.make_async_copy(pert_ref.at[:, :, pl.ds(mine, half)], pert, local_sem.at[3]),
    ]

    barrier = pltpu.get_barrier_semaphore()
    for q, t in relations[1:]:
        pl.semaphore_signal(
            barrier, inc=1, device_id={"mem": target(q, t)}, device_id_type=MESH_ID
        )

    def toward(semaphore, up, t):
        @pl.when(lon < ring - 1 if up else lon > 0)
        def _():
            pl.semaphore_signal(
                semaphore,
                inc=1,
                device_id={"lon": east if up else west, "mem": target(0, t)},
                device_id_type=MESH_ID,
            )

    for t in range(2):
        toward(barrier, True, t)
        toward(barrier, False, t)
    for copy in local:
        copy.start()
    line = lax.broadcasted_iota(jnp.int32, (EDGE, lat), 0)
    ids[mem] = jnp.where(line == 0, anc_ref[0], sel_ref[0])
    beside = jnp.where(lon > 0, 1, 0) + jnp.where(lon < ring - 1, 1, 0)
    pl.semaphore_wait(barrier, n - 1 + 2 * beside)

    def pass_token(up):
        pl.semaphore_wait(token.at[int(up)], 1)
        toward(token.at[int(up)], up, 0)

    def send_ids(q, t):
        slot = 2 * q + t - 1
        return pltpu.make_async_remote_copy(
            src_ref=ids.at[mem],
            dst_ref=ids.at[mem],
            send_sem=i_send.at[slot],
            recv_sem=i_recv.at[slot],
            device_id={"mem": target(q, t)},
            device_id_type=MESH_ID,
        )

    to_twin = pltpu.make_async_remote_copy(
        src_ref=init_ref.at[0, :, pl.ds(half - mine, half)],
        dst_ref=state.at[core],
        send_sem=p_send,
        recv_sem=p_recv,
        device_id={"mem": target(0, 1)},
        device_id_type=MESH_ID,
    )

    def lon_copy(source, place, slot, side, t=0):
        return pltpu.make_async_remote_copy(
            src_ref=source,
            dst_ref=place,
            send_sem=z_send.at[slot, side],
            recv_sem=z_recv.at[slot, side],
            device_id={"lon": jnp.where(side == 1, east, west), "mem": target(0, t)},
            device_id_type=MESH_ID,
        )

    def edge_rows(w):
        return pl.ds(pl.multiple_of(top * w, EDGE), EDGE)

    def beyond(w):
        return pl.ds(pl.multiple_of(2 * EDGE * w, EDGE), EDGE)

    dyn = fields - 1

    def halo(t, side, humid=False):
        which = pl.ds(dyn, 1) if humid else pl.ds(0, dyn)
        return lon_copy(
            init_ref.at[0, which, pl.ds(core_of(t) * half, half), edge_rows(side)],
            frame.at[1 - side, core, which, :, beyond(1 - side)],
            4 + t if humid else t,
            side,
            t,
        )

    def kap_copy(side):
        return lon_copy(
            kap_ref.at[pl.ds(mine, half), edge_rows(side)],
            kap_frame.at[1 - side, :, beyond(1 - side)],
            2,
            side,
        )

    def pert_copy(side):
        return lon_copy(pert_edge.at[side], pert_halo.at[1 - side], 3, side)

    def start_halo(side):
        halo(0, side).start()
        halo(1, side).start()
        kap_copy(side).start()

    def start_rims(side):
        pert_copy(side).start()
        halo(0, side, True).start()
        halo(1, side, True).start()

    for q, t in relations[2:] + relations[1:2]:
        send_ids(q, t).start()
    to_twin.start()
    for side, inside in enumerate((lon > 0, lon < ring - 1)):

        @pl.when(inside)
        def _():
            start_halo(side)

    lower = jnp.logical_and(lon > 0, 2 * lon < ring)
    upper = 2 * lon >= ring

    @pl.when(lon == 1)
    def _():
        toward(token.at[1], True, 0)

    @pl.when(lon == ring - 2)
    def _():
        toward(token.at[0], False, 0)

    @pl.when(jnp.logical_and(lower, lon > 1))
    def _():
        pass_token(True)

    lane = lax.broadcasted_iota(jnp.int32, (width, lat), 1)
    not_north = jnp.where(lane == lat - 1, 0.0, 1.0)
    not_south = jnp.where(lane == 0, 0.0, 1.0)

    def from_west(q):
        return pltpu.roll(q, 1, 0)

    def from_east(q):
        return pltpu.roll(q, q.shape[0] - 1, 0)

    def from_south(q):
        return pltpu.roll(q, 1, 1)

    def from_north(q):
        return pltpu.roll(q, lat - 1, 1)

    def put_faces(held, level, k):
        to_east = (0.5 * TIME_STEP) * (k + from_east(k))
        to_north = (0.5 * TIME_STEP) * (k + from_north(k)) * not_north[: k.shape[0]]
        held[0, level] = to_east
        held[1, level] = from_west(to_east)
        held[2, level] = to_north
        held[3, level] = from_south(to_north)

    def coefficients(u, v, held, level):
        size = u.shape[0]
        u = TIME_STEP * u
        v = TIME_STEP * v
        to_e = held[0, level] - jnp.minimum(u, 0.0)
        to_w = held[1, level] + jnp.maximum(u, 0.0)
        to_n = held[2, level] - jnp.minimum(v, 0.0) * not_north[:size]
        to_s = held[3, level] + jnp.maximum(v, 0.0) * not_south[:size]
        here = 1.0 - ((to_e + to_w) + (to_n + to_s))
        return to_e, to_w, to_n, to_s, here

    def moved(q, c):
        to_e, to_w, to_n, to_s, here = c
        return (
            here * q
            + (to_e * from_east(q) + to_w * from_west(q))
            + (to_n * from_north(q) + to_s * from_south(q))
        )

    def observed(t, share):
        terms = share * t * t
        return jnp.sum(terms.reshape(-1, 8, lat), axis=0)

    def look_inner(t):
        return observed(t[EDGE:top], weight[EDGE:top])

    def advance(states, held, spots, totals, look, keep=None):
        for step in range(STEPS):
            for k in range(len(states)):
                c = coefficients(states[k][0], states[k][1], held, spots[k])
                if keep is not None:
                    for i in range(5):
                        keep[k, step, i] = c[i]
                states[k] = [moved(q, c) for q in states[k]]
                totals[k] = totals[k] + look(states[k][2])
        return states, totals

    zero = jnp.zeros((8, lat), jnp.float32)

    def inner_member(t):
        a = core_of(t)
        states = [[state[a, f, level] for f in range(fields)] for level in range(half)]
        states, totals = advance(states, face, list(range(half)), [zero] * half, look_inner)
        for level in range(half):
            for f in range(fields):
                mid[a, f, level] = states[level][f]
        acc[t, 0] = functools.reduce(jnp.add, totals)

    for copy in local[:3]:
        copy.wait()
    for level in range(half):
        put_faces(face, level, kap[level])
    inner_member(0)

    kinds = pert.shape[0]
    packed = pert_edge.shape[2]
    used = half * fields * STEPS
    local[3].wait()

    def pack(j, carry):
        for level in range(half):
            for f in range(fields):
                spot = pl.ds((level * fields + f) * STEPS, STEPS)
                pert_edge[0, j, spot, :] = pert[j, f, level, 0:STEPS, :]
                pert_edge[1, j, spot, :] = pert[j, f, level, width - STEPS : width, :]
        if packed > used:
            for side in range(2):
                pert_edge[side, j, pl.ds(used, packed - used), :] = jnp.zeros(
                    (packed - used, lat), jnp.float32
                )
        return carry

    lax.fori_loop(0, kinds, pack, 0)
    for side, inside in enumerate((lon > 0, lon < ring - 1)):

        @pl.when(inside)
        def _():
            start_rims(side)

    @pl.when(upper)
    def _():
        pass_token(True)

        @pl.when(lon < ring - 2)
        def _():
            pass_token(False)

        @pl.when(lon == ring - 1)
        def _():
            start_halo(1)
            start_rims(1)

    @pl.when(lower)
    def _():
        pass_token(False)

    to_twin.wait_recv()
    inner_member(1)


    def choose(q, t, level):
        chosen = ids[target(q, t), 1:2, :]
        for f in range(fields):
            value = pert[0, f, level]
            for j in range(1, kinds):
                value = jnp.where(chosen == j, pert[j, f, level], value)
            noise[2 * q + t, f, level] = value

    def piece(q, t, slot, levels_here, levels_there, rows):
        r = 2 * q + t
        return pltpu.make_async_remote_copy(
            src_ref=stage.at[r, :, levels_here, rows],
            dst_ref=res_ref.at[pair, :, levels_there, rows],
            send_sem=x_send.at[r - 1, slot],
            recv_sem=x_recv.at[r - 1, slot],
            device_id={"mem": target(q, t)},
            device_id_type=MESH_ID,
        )

    def inner_piece(q, t, level):
        return piece(q, t, level, level, mine + level, pl.ds(EDGE, top - EDGE))

    def outer_piece(q, t, w):
        return piece(q, t, half + w, pl.ds(0, half), pl.ds(mine, half), edge_rows(w))

    def put(q, t, f, level, rows, value):
        if (q, t) == (0, 0):
            res_ref[pair, f, mine + level, rows, :] = value
        else:
            stage[2 * q + t, f, level, rows, :] = value

    def second(q, t):
        return ids[target(q, t), 0:1, :] == base + 1

    def inner_clones(q):
        def one(level, totals):
            totals = list(totals)
            for t in range(2):
                if (q, t) != (0, 0):

                    @pl.when(level == 0)
                    def _():
                        send_ids((pairs - q) % pairs, t).wait_recv()

                choose(q, t, level)
                states = [
                    [
                        jnp.where(second(q, t), mid[1, f, level], mid[0, f, level])
                        + noise[2 * q + t, f, level]
                        for f in range(fields)
                    ]
                ]
                states, (totals[t],) = advance(states, face, [level], [totals[t]], look_inner)
                for f in range(fields):
                    put(q, t, f, level, slice(EDGE, top), states[0][f][EDGE:top])
                if (q, t) != (0, 0):
                    inner_piece(q, t, level).start()
            if q == 1:

                @pl.when(jnp.logical_and(lon == 0, level == 0))
                def _():
                    pl.semaphore_wait(token.at[0], 1)
                    start_halo(0)
                    start_rims(0)

            return tuple(totals)

        totals = lax.fori_loop(0, half, one, (zero, zero))
        for t in range(2):
            acc[2 * q + t, 1] = totals[t]

    for q in range(1, pairs):
        inner_clones(q)

    inner_clones(0)

    blank = jnp.zeros((EDGE - STEPS, lat), jnp.float32)
    spots = [(level, t) for level in range(half) for t in range(2)]

    def outer_rows(turn, carry):
        w = jnp.where(lon == 0, 1 - turn, turn)
        here = pl.ds(pl.multiple_of(EDGE * (1 - w), EDGE), 2 * EDGE)
        there = pl.ds(pl.multiple_of((width - 2 * EDGE) * w, EDGE), 2 * EDGE)

        def look_outer(t):
            return observed(t[EDGE : 2 * EDGE], weight[edge_rows(w)])

        kap_copy(1 - w).wait_recv()
        halo(0, 1 - w).wait_recv()
        halo(1, 1 - w).wait_recv()

        states = []
        for level in range(half):
            kap_frame[w, level, here, :] = kap[level, there, :]
            put_faces(face_e, level, kap_frame[w, level])
        for level, t in spots:
            for f in range(dyn):
                frame[w, core_of(t), f, level, here, :] = state[core_of(t), f, level, there, :]
            states.append([frame[w, core_of(t), f, level] for f in range(dyn)])
        grounds = [level for level, _ in spots]
        nothing = [zero] * len(spots)
        states, totals = advance(states, face_e, grounds, list(nothing), look_outer, coef_m.at[w])
        for (level, t), fresh, total_of in zip(spots, states, totals):
            for f in range(dyn):
                mid_e[core_of(t), f, level] = fresh[f]
            acc[t, 0] = acc[t, 0] + total_of
        pert_copy(1 - w).wait_recv()

        for q in list(range(1, pairs)) + [0]:
            states = []
            for level, t in spots:
                r = 2 * q + t
                chosen = ids[target(q, t), 1:2, :]
                ends = pert_halo[w, 0]
                for j in range(1, kinds):
                    ends = jnp.where(chosen == j, pert_halo[w, j], ends)
                fresh = []
                for f in range(dyn):
                    start = (level * fields + f) * STEPS
                    rim = ends[start : start + STEPS]
                    noise_e[level, t, f, here, :] = noise[r, f, level, there, :]
                    noise_e[level, t, f, beyond(w), :] = jnp.where(
                        w == 0,
                        jnp.concatenate([blank, rim], axis=0),
                        jnp.concatenate([rim, blank], axis=0),
                    )
                    fresh.append(
                        jnp.where(second(q, t), mid_e[1, f, level], mid_e[0, f, level])
                        + noise_e[level, t, f]
                    )
                states.append(fresh)
            states, totals = advance(
                states, face_e, grounds, list(nothing), look_outer, coef_c.at[w, q]
            )
            for (level, t), fresh, total_of in zip(spots, states, totals):
                for f in range(dyn):
                    put(q, t, f, level, edge_rows(w), fresh[f][EDGE : 2 * EDGE])
                acc[2 * q + t, 1] = acc[2 * q + t, 1] + total_of
        return carry

    lax.fori_loop(0, 2, outer_rows, 0)
    for q, t in relations:
        r = 2 * q + t
        ancestor = ids[target(q, t), 0:1, :]
        held = jnp.logical_or(ancestor == base, ancestor == base + 1)
        acc[r, 1] = jnp.where(held, acc[r, 1], 0.0)
        if q:
            acc[r, 0] = zero

    block[...] = jnp.concatenate(
        [
            jnp.sum(acc[2 * q + t, which], axis=0, keepdims=True)
            for q, t in relations
            for which in range(2)
        ],
        axis=0,
    )
    spread[lon] = block[...]
    shares = [
        pltpu.make_async_remote_copy(
            src_ref=block,
            dst_ref=spread.at[lon],
            send_sem=s_send.at[d - 1],
            recv_sem=s_recv.at[d - 1],
            device_id={"lon": lax.rem(lon + d, ring)},
            device_id_type=MESH_ID,
        )
        for d in range(1, ring)
    ]
    for copy in shares:
        copy.start()

    def glide(values, kept):
        for step in range(STEPS):
            for k in range(len(values)):
                values[k] = moved(values[k], [kept[k][step, i] for i in range(5)])
        return values

    places = [(w, x) for w in range(2) for x in range(len(spots))]
    values = []
    for w, x in places:
        level, t = spots[x]
        if x == 0:
            for side_t in range(2):
                halo(side_t, 1 - w, True).wait_recv()
        shore = pl.ds((width - 2 * EDGE) * w, 2 * EDGE)
        own_rows = state[core_of(t), dyn, level, shore, :]
        rim = frame[w, core_of(t), dyn, level, 2 * EDGE * w : 2 * EDGE * w + EDGE, :]
        values.append(jnp.concatenate([own_rows, rim] if w else [rim, own_rows], axis=0))
    values = glide(values, [coef_m.at[w, x] for w, x in places])
    for (w, x), value in zip(places, values):
        level, t = spots[x]
        mid_h[w, core_of(t), level] = value
    for q in list(range(1, pairs)) + [0]:
        values = []
        for w, x in places:
            level, t = spots[x]
            chosen = ids[target(q, t), 1:2, :]
            start = (level * fields + dyn) * STEPS
            rim = pert_halo[w, 0, start : start + STEPS, :]
            for j in range(1, kinds):
                rim = jnp.where(chosen == j, pert_halo[w, j, start : start + STEPS, :], rim)
            shore = pl.ds((width - 2 * EDGE) * w, 2 * EDGE)
            own_rows = noise[2 * q + t, dyn, level, shore, :]
            parts = [own_rows, rim, blank] if w else [blank, rim, own_rows]
            values.append(
                jnp.where(second(q, t), mid_h[w, 1, level], mid_h[w, 0, level])
                + jnp.concatenate(parts, axis=0)
            )
        values = glide(values, [coef_c.at[w, q, x] for w, x in places])
        for (w, x), value in zip(places, values):
            level, t = spots[x]
            put(q, t, dyn, level, edge_rows(w), value[EDGE : 2 * EDGE])
        for t in range(2):
            if (q, t) != (0, 0):
                outer_piece(q, t, 0).start()
                if (q, t) != (pairs - 1, 1):
                    outer_piece(q, t, 1).start()

    for q, t in relations[1:]:
        send_ids(q, t).wait_send()
    for side in range(2):
        kap_copy(side).wait_send()
        pert_copy(side).wait_send()
        for t in range(2):
            halo(t, side).wait_send()
            halo(t, side, True).wait_send()
    to_twin.wait_send()
    for copy in shares:
        copy.wait_recv()

    def hand(q, t):
        r = 2 * q + t
        return pltpu.make_async_remote_copy(
            src_ref=total,
            dst_ref=gather.at[r],
            send_sem=g_send.at[r - 1],
            recv_sem=g_recv.at[r - 1],
            device_id={"mem": target(q, t)},
            device_id_type=MESH_ID,
        )

    whole = jnp.sum(spread[...], axis=0)
    total[...] = whole
    gather[0] = whole
    for q, t in relations[1:]:
        hand(q, t).start()
    outer_piece(pairs - 1, 1, 1).start()
    for copy in shares:
        copy.wait_send()
    for q, t in relations[1:]:
        for level in range(half):
            inner_piece(q, t, level).wait()
    for q, t in relations[1:]:
        for w in range(2):
            outer_piece(q, t, w).wait()
    for q, t in relations[1:]:
        hand(q, t).wait_send()
    for q, t in relations[1:]:
        hand(q, t).wait_recv()
    cells = levels * lat * width * ring
    pair_of = functools.reduce(jnp.add, [gather[r, 2 * r : 2 * r + 2, :] for r in range(n)])
    summed = jnp.sum(pair_of, axis=1, keepdims=True) / cells
    column = lax.broadcasted_iota(jnp.int32, (1, 2), 1)
    act_ref[...] = jnp.where(column == 0, summed[0:1], summed[1:2])


def finish(anc_ref, res_ref, action_ref, state_out, action_out, sem):
    fields = res_ref.shape[1]
    chosen = anc_ref[0] // 2
    copies = [
        pltpu.make_async_copy(res_ref.at[chosen, f], state_out.at[0, f], sem.at[f])
        for f in range(fields)
    ]
    copies.append(pltpu.make_async_copy(action_ref, action_out, sem.at[fields]))
    for copy in copies:
        copy.start()
    for copy in copies:
        copy.wait()


def body(initial_state, ancestor, selector, perturbations, diffusivity, region_weight):
    n, ring = lax.axis_size("mem"), lax.axis_size("lon")
    _, fields, levels, width, lat = initial_state.shape
    half, pairs = levels // 2, n // 2
    kinds = perturbations.shape[0]
    outer = 3 * EDGE
    packed = -(-half * fields * STEPS // 8) * 8
    f32 = jnp.float32
    far = pl.BlockSpec(memory_space=pltpu.HBM)
    near = pl.BlockSpec(memory_space=pltpu.VMEM)
    scalar = pl.BlockSpec(memory_space=pltpu.SMEM)
    dma = pltpu.SemaphoreType.DMA
    results, action = pl.pallas_call(
        functools.partial(kernel, n, ring),
        out_shape=(
            pltpu.VMEM((pairs, fields, levels, width, lat), f32),
            pltpu.VMEM((1, 2), f32),
        ),
        in_specs=[scalar] * 2 + [far] * 4,
        out_specs=(near,) * 2,
        scratch_shapes=[
            pltpu.VMEM((2, fields, half, width, lat), f32),
            pltpu.VMEM((2, 2, fields, half, outer, lat), f32),
            pltpu.VMEM((2, fields, half, width, lat), f32),
            pltpu.VMEM((2, fields, half, outer, lat), f32),
            pltpu.VMEM((half, width, lat), f32),
            pltpu.VMEM((2, half, outer, lat), f32),
            pltpu.VMEM((4, half, width, lat), f32),
            pltpu.VMEM((4, half, outer, lat), f32),
            pltpu.VMEM((kinds, fields, half, width, lat), f32),
            pltpu.VMEM((n, fields, half, width, lat), f32),
            pltpu.VMEM((half, 2, fields - 1, outer, lat), f32),
            pltpu.VMEM((2, 2, half, outer, lat), f32),
            pltpu.VMEM((2, 2 * half, STEPS, 5, outer, lat), f32),
            pltpu.VMEM((2, pairs, 2 * half, STEPS, 5, outer, lat), f32),
            pltpu.VMEM((2, kinds, packed, lat), f32),
            pltpu.VMEM((2, kinds, packed, lat), f32),
            pltpu.VMEM((n, fields, half, width, lat), f32),
            pltpu.VMEM((width, lat), f32),
            pltpu.VMEM((n, EDGE, lat), jnp.int32),
            pltpu.VMEM((n, 2, 8, lat), f32),
            pltpu.VMEM((2 * n, lat), f32),
            pltpu.VMEM((ring, 2 * n, lat), f32),
            pltpu.VMEM((2 * n, lat), f32),
            pltpu.VMEM((n, 2 * n, lat), f32),
            dma((n - 1,)),
            dma((n - 1,)),
            dma,
            dma,
            dma((6, 2)),
            dma((6, 2)),
            dma((n - 1, half + 2)),
            dma((n - 1, half + 2)),
            dma((n - 1,)),
            dma((n - 1,)),
            dma((ring - 1,)),
            dma((ring - 1,)),
            dma((4,)),
            pltpu.SemaphoreType.REGULAR((2,)),
        ],
        compiler_params=pltpu.CompilerParams(
            collective_id=0, has_side_effects=True, vmem_limit_bytes=VMEM_LIMIT
        ),
    )(ancestor, selector, initial_state, perturbations, diffusivity, region_weight)
    return pl.pallas_call(
        finish,
        out_shape=(
            jax.ShapeDtypeStruct(initial_state.shape, f32),
            jax.ShapeDtypeStruct((1, 2), f32),
        ),
        in_specs=[scalar, near, near],
        out_specs=(far,) * 2,
        scratch_shapes=[dma((fields + 1,))],
        compiler_params=pltpu.CompilerParams(vmem_limit_bytes=1 << 20),
    )(ancestor, results, action)


def solution(mesh):
    in_specs = (
        P(("ens", "mem"), None, None, "lon", None),
        P(("ens", "mem")),
        P(("ens", "mem")),
        P("ens", None, None, "lon", None),
        P(None, "lon", None),
        P("lon", None),
    )
    out_specs = (P(("ens", "mem"), None, None, "lon", None), P(("ens", "mem"), None))
    return jax.shard_map(body, mesh=mesh, in_specs=in_specs, out_specs=out_specs, check_vma=False)
```
